256 devices in a mesh: tm: 16 (over x, y), space: 16 (over z, core).
Axes of the slice: x: 4, y: 4, z: 8, core: 2. Of those that a mesh axis runs over, the one named last changes fastest.
Arguments:
- initial: float32 [3, 64, 16, 128], P(None, 'space'), may hold values from -4 to 4
- guesses: float32 [64, 3, 64, 16, 128], P('tm', None, 'space'), may hold values from -4 to 4
- viscosity: float32 [64, 16, 128], P('space'), may hold values from 0.5 to 1
- forcing: float32 [3, 64, 16, 128], P(None, 'space'), may hold values from -6 to 6, as said below
Outputs:
- solution: float32 [256, 3, 64, 16, 128], P('tm', None, 'space')
The draws below stay inside these ranges and needn't reach their ends.
Inputs may be any that keep to these rules, and one draw needn't show every extreme that they name: `forcing`: a body force for each cell and component.
All inputs are finite; a program needn't handle non-finite values.
Results may differ from the reference program's by a relative error of at most 0.00002.
Values sent between devices are 32-bit elements; how exact they have to be, the bound alone decides.
No kernel may reach another device: no remote copies, remote signals or barrier semaphores. Data moves between devices by JAX's collectives and lax.ppermute only.
A program may use at most 64 MiB of HBM per device.

```python
import math
import jax
import jax.numpy as jnp
from jax import lax

NY = 16
NX = 128
NZ = 64
NC = 64


def draw_forcing(key, part):
    jagged = jnp.clip(jax.random.normal(key, (3, NZ, NY, NX), jnp.float32), -4.0, 4.0)
    return jagged


def level_of(key, shape, cuts, least, largest):
    level = 1.0
    for axis_at, shards_of in cuts:
        draws = jax.random.uniform(jax.random.fold_in(jax.random.fold_in(key, 6), axis_at), (shards_of,), jnp.float32, least / len(cuts), largest / len(cuts))
        level = level * jnp.repeat(jnp.exp(draws), shape[axis_at] // shards_of).reshape((-1,) + (1,) * (len(shape) - 1 - axis_at))
    return level


def normal_values(key, shape, width, reach, shards=(), kind=jnp.bfloat16):
    level = level_of(key, shape, shards, -0.22, 0.18) if shards else 1.0
    values = jax.random.normal(key, shape, jnp.float32) * width * level
    return jnp.minimum(jnp.maximum(values, -reach), reach).astype(kind)


def setup_inputs(seed: int = 0) -> dict:
    streams_of = jax.random.split(jax.random.key(seed), 5)
    initial = normal_values(streams_of[0], (3, NZ, NY, NX), 0.5, 4.0, ((1, 16),), jnp.float32)
    guesses = normal_values(streams_of[1], (NC, 3, NZ, NY, NX), 0.7, 4.0, ((0, 16), (2, 16)), jnp.float32)
    viscosity = jnp.clip(jnp.exp(math.log(1.0) - 0.6931472 * jax.random.uniform(streams_of[2], (NZ, NY, NX), jnp.float32) ** level_of(streams_of[2], (NZ, NY, NX), ((0, 16),), -0.2, 0.2)), 0.5, 1.0)
    forcing = draw_forcing(jax.random.fold_in(streams_of[4], 71), 0)
    return {"initial": initial, "guesses": guesses, "viscosity": viscosity, "forcing": forcing}


time_step = 0.019


def wrap_planes(array, axis):
    extent = array.shape[axis]
    return jnp.concatenate([lax.slice_in_dim(array, extent - 1, extent, axis=axis), array, lax.slice_in_dim(array, 0, 1, axis=axis)], axis=axis)


def substep(padded, fields, step_size):
    center = padded[:, :, 1:-1]
    plane_up = padded[:, :, 2:]
    plane_down = padded[:, :, :-2]
    cell_east = jnp.roll(center, -1, axis=4)
    cell_west = jnp.roll(center, 1, axis=4)
    cell_north = jnp.roll(center, -1, axis=3)
    cell_south = jnp.roll(center, 1, axis=3)
    slope_x = (cell_east - cell_west) * 0.5
    slope_y = (cell_north - cell_south) * 0.5
    slope_z = (plane_up - plane_down) * 0.5
    spread = cell_east + cell_west + cell_north + cell_south + plane_up + plane_down - 6.0 * center
    carried = center[:, 0:1] * slope_x + center[:, 1:2] * slope_y + center[:, 2:3] * slope_z
    viscous = fields[None, 0:1, 1:-1]
    pushed = fields[None, 1:4, 1:-1]
    return center + step_size * (viscous * spread - carried + pushed)


def propagate(current, fields, step_size, substeps):
    for repeat in range(substeps):
        current = substep(wrap_planes(current, 2), fields, step_size)
    return current


def reference(initial, guesses, viscosity, forcing):
    fields = wrap_planes(jnp.concatenate([viscosity[None], forcing], axis=0), 1)

    def fine_step(current):
        return propagate(current, fields, time_step, 1)

    def middle_step(current):
        return propagate(current, fields, 2.0 * time_step, 2)

    def coarse_step(current):
        return propagate(current, fields, 8.0 * time_step, 2)

    blocks = guesses.shape[0] // 4
    grouped = guesses.reshape((blocks, 4) + guesses.shape[1:])
    openings = jnp.concatenate([initial[None], grouped[:-1, 3]], axis=0)

    def prepare(inputs_pair):
        opening, members = inputs_pair
        starts = jnp.concatenate([opening[None], members[:-1]], axis=0)
        current = starts
        for repeat in range(4):
            current = fine_step(current)
        rhs_one = current - middle_step(starts)
        level_value = opening[None]
        for station in range(3):
            level_value = middle_step(level_value) + rhs_one[station:station + 1]
        rhs_two = middle_step(level_value) + rhs_one[3:4] - coarse_step(opening[None])
        return rhs_one, rhs_two[0]

    rhs_ones, rhs_twos = lax.map(prepare, (openings, grouped))

    def march(marching, rhs_two):
        stepped = coarse_step(marching[None])[0] + rhs_two
        return stepped, (marching, stepped)

    last_state, (start_states, end_states) = lax.scan(march, initial, rhs_twos)

    def finish_block(inputs_triple):
        interval_start, interval_end, rhs_one = inputs_triple
        level_value = interval_start[None]
        values = []
        for station in range(3):
            level_value = middle_step(level_value) + rhs_one[station:station + 1]
            values.append(level_value)
        targets = jnp.concatenate(values + [interval_end[None]], axis=0)
        anchors = jnp.concatenate([interval_start[None]] + values, axis=0)
        fine_one = fine_step(anchors)
        fine_two = fine_step(fine_one)
        fine_three = fine_step(fine_two)
        result = jnp.stack([fine_one, fine_two, fine_three, targets], axis=1)
        return result.reshape((16,) + targets.shape[1:])

    solution = lax.map(finish_block, (start_states, end_states, rhs_ones))
    return solution.reshape((blocks * 16,) + initial.shape)
```

```python
import functools

import jax
import jax.numpy as jnp
from jax import lax
from jax.experimental import pallas as pl
from jax.experimental.pallas import tpu as pltpu
from jax.sharding import PartitionSpec as P

time_step = 0.019
FINE, MIDDLE, COARSE = time_step, 2.0 * time_step, 8.0 * time_step
DEPTH = 4
AXES = ("tm", "space")


def slab(low, own, high, *lead):
    def get(c, z):
        if z < 0:
            return low[(*lead, c, z + DEPTH)]
        if z >= DEPTH:
            return high[(*lead, c, z - DEPTH)]
        return own[(*lead, c, z)]

    return get


def reader(ref, shift=DEPTH):
    return lambda c, z: ref[c, z + shift]


def writer(ref, shift=DEPTH):
    def put(c, z, value):
        ref[c, z + shift] = value

    return put


def advance(get, put, first, last, table, step_size):
    for z in range(first, last):
        alpha = table[0, z + DEPTH]
        keep = table[1, z + DEPTH]
        center = [get(c, z) for c in range(3)]
        half = [value * (0.5 * step_size) for value in center]
        east, west = alpha - half[0], alpha + half[0]
        north, south = alpha - half[1], alpha + half[1]
        up, down = alpha - half[2], alpha + half[2]
        for c in range(3):
            value = center[c]
            along_x = east * pltpu.roll(value, 127, 1) + west * pltpu.roll(value, 1, 1)
            along_y = north * pltpu.roll(value, 15, 0) + south * pltpu.roll(value, 1, 0)
            along_z = up * get(c, z + 1) + down * get(c, z - 1)
            put(c, z, (keep * value + table[2 + c, z + DEPTH]) + along_x + (along_y + along_z))


def tables_kernel(low, own, high, fine, middle, coarse):
    get = slab(low, own, high)
    for table, step_size in ((fine, FINE), (middle, MIDDLE), (coarse, COARSE)):
        for z in range(-DEPTH, 2 * DEPTH):
            alpha = get(0, z) * step_size
            table[0, z + DEPTH] = alpha
            table[1, z + DEPTH] = 1.0 - 6.0 * alpha
            for c in range(3):
                table[2 + c, z + DEPTH] = get(1 + c, z) * step_size


def defects_kernel(low, own, high, fine, middle, out, one, two):
    def body(i, carry):
        start = slab(low, own, high, i)
        advance(start, writer(one), -3, 7, fine, FINE)
        advance(reader(one), writer(two), -2, 6, fine, FINE)
        advance(reader(two), writer(one), -1, 5, fine, FINE)

        def store(c, z, value):
            out[i, c, z] = value

        def subtract(c, z, value):
            out[i, c, z] = out[i, c, z] - value

        advance(reader(one), store, 0, 4, fine, FINE)
        advance(start, writer(two), -1, 5, middle, MIDDLE)
        advance(reader(two), subtract, 0, 4, middle, MIDDLE)
        return carry

    lax.fori_loop(0, own.shape[0], body, 0)


def opening_kernel(low, own, high, fine, defects, to_up, to_down, one, two):
    advance(slab(low, own, high), writer(one), -3, 7, fine, FINE)
    advance(reader(one), writer(two), -2, 6, fine, FINE)
    advance(reader(two), writer(one), -1, 5, fine, FINE)

    def store(c, z, value):
        to_up[c, z] = value
        to_down[c, z] = value

    advance(reader(one), store, 0, 4, fine, FINE)
    for c in range(3):
        for z in range(2):
            to_up[c, 4 + z] = defects[0, c, 2 + z]
            to_down[c, 4 + z] = defects[0, c, z]


def remainder_kernel(low, own, high, middle, coarse, defects, first, defect, rest, one):
    start = slab(low, own, high)
    advance(start, writer(one), -1, 5, middle, MIDDLE)

    def subtract(c, z, value):
        defect[c, z] = first[c, z] - value

    advance(reader(one), subtract, 0, 4, middle, MIDDLE)
    advance(start, writer(one), -1, 5, coarse, COARSE)

    def subtract_rest(c, z, value):
        rest[c, z] = defects[2, c, z] - value

    advance(reader(one), subtract_rest, 0, 4, coarse, COARSE)


def second_kernel(low, own, high, middle, defects, defect, rest, to_up, to_down, one, two):
    def added(c, z, value):
        if z < 0:
            term = low[c, 4 + 2 + z]
        elif z >= DEPTH:
            term = high[c, 4 + z - DEPTH]
        else:
            term = defects[0, c, z]
        two[c, z + DEPTH] = value + term

    def third(c, z, value):
        value = value + defects[1, c, z]
        to_up[c, z] = value
        to_down[c, z] = value

    advance(slab(low, own, high), writer(one), -3, 7, middle, MIDDLE)
    advance(reader(one), added, -2, 6, middle, MIDDLE)
    advance(reader(two), writer(one), -1, 5, middle, MIDDLE)
    advance(reader(one), third, 0, 4, middle, MIDDLE)
    for c in range(3):
        for z in range(2):
            to_up[c, 4 + z] = rest[c, 2 + z]
            to_down[c, 4 + z] = rest[c, z]
            to_up[c, 6 + z] = defect[c, 2 + z]
            to_down[c, 6 + z] = defect[c, z]


def coarse_defect_kernel(low, own, high, middle, rest, out, one):
    def added(c, z, value):
        if z < 0:
            term = low[c, 4 + 2 + z]
        elif z >= DEPTH:
            term = high[c, 4 + z - DEPTH]
        else:
            term = rest[c, z]
        out[c, z + 2] = value + term

    advance(slab(low, own, high), writer(one), -3, 7, middle, MIDDLE)
    advance(reader(one), added, -2, 6, middle, MIDDLE)


def march_kernel(low, own, high, coarse, term_one, term_two, out_one, out_two, one, two):
    def first(c, z, value):
        value = value + term_one[c, z + 2]
        two[c, z + DEPTH] = value
        if 0 <= z < DEPTH:
            out_one[c, z] = value

    def second(c, z, value):
        out_two[c, z] = value + term_two[c, z + 2]

    advance(slab(low, own, high), writer(one), -3, 7, coarse, COARSE)
    advance(reader(one), first, -2, 6, coarse, COARSE)
    advance(reader(two), writer(one), -1, 5, coarse, COARSE)
    advance(reader(one), second, 0, 4, coarse, COARSE)


def last_march_kernel(low, own, high, coarse, term_one, out_one, one):
    def first(c, z, value):
        out_one[c, z] = value + term_one[c, z + 2]

    advance(slab(low, own, high), writer(one), -1, 5, coarse, COARSE)
    advance(reader(one), first, 0, 4, coarse, COARSE)


def stations_kernel(low, own, high, middle, defect_low, defect, defect_high, defects, out, one, two):
    def first(c, z, value):
        if z < 0:
            term = defect_low[c, 6 + 2 + z]
        elif z >= DEPTH:
            term = defect_high[c, 6 + z - DEPTH]
        else:
            term = defect[c, z]
        value = value + term
        two[c, z + DEPTH] = value
        if 0 <= z < DEPTH:
            out[0, c, z] = value

    def second(c, z, value):
        out[1, c, z] = value + defects[0, c, z]

    advance(slab(low, own, high), writer(one), -3, 7, middle, MIDDLE)
    advance(reader(one), first, -2, 6, middle, MIDDLE)
    advance(reader(two), writer(one), -1, 5, middle, MIDDLE)
    advance(reader(one), second, 0, 4, middle, MIDDLE)


def third_kernel(low, own, high, middle, defects, out, one):
    def third(c, z, value):
        out[c, z] = value + defects[1, c, z]

    advance(slab(low, own, high, 1), writer(one), -1, 5, middle, MIDDLE)
    advance(reader(one), third, 0, 4, middle, MIDDLE)


def fine_rows(start, fine, rows, at, one, two):
    def first(c, z, value):
        one[c, z + DEPTH] = value
        if 0 <= z < DEPTH:
            rows[at, c, z] = value

    def second(c, z, value):
        two[c, z + DEPTH] = value
        if 0 <= z < DEPTH:
            rows[at + 1, c, z] = value

    def third(c, z, value):
        rows[at + 2, c, z] = value

    advance(start, first, -2, 6, fine, FINE)
    advance(reader(one), second, -1, 5, fine, FINE)
    advance(reader(two), third, 0, 4, fine, FINE)


def send_rows(rows, result, sem, places):
    copies = [
        pltpu.make_async_copy(rows.at[at], result.at[place], sem.at[at])
        for at, place in enumerate(places)
    ]
    for copy in copies:
        copy.start()
    for copy in copies:
        copy.wait()


def first_rows_kernel(low, own, high, fine, coarse, term, stations, result, rows, one, two, sem):
    start = slab(low, own, high)
    fine_rows(start, fine, rows, 0, one, two)
    for c in range(3):
        for z in range(DEPTH):
            rows[3, c, z] = stations[0, c, z]
            rows[4, c, z] = stations[1, c, z]

    def end(c, z, value):
        rows[5, c, z] = value + term[c, z + 2]

    advance(start, writer(one), -1, 5, coarse, COARSE)
    advance(reader(one), end, 0, 4, coarse, COARSE)
    send_rows(rows, result, sem, (0, 1, 2, 3, 7, 15))


def middle_rows_kernel(low, own, high, fine, station, before, result, rows, one, two, sem):
    for i in range(2):
        fine_rows(slab(low, own, high, i), fine, rows, 3 * i, one, two)
    for c in range(3):
        for z in range(DEPTH):
            rows[6, c, z] = station[c, z]
    send_rows(rows, result, sem, (4, 5, 6, 8, 9, 10, 11))


def last_rows_kernel(low, own, high, fine, before, result, rows, one, two, sem):
    fine_rows(slab(low, own, high), fine, rows, 0, one, two)
    send_rows(rows, result, sem, (12, 13, 14))


def ring(x, by, columns):
    spaces = lax.axis_size("space")
    pairs = [(t * spaces + s, t * spaces + (s + by) % spaces) for t in columns for s in range(spaces)]
    return lax.ppermute(x, AXES, pairs)


def halos(to_up, to_down, columns):
    return ring(to_up, 1, columns), ring(to_down, -1, columns)


def move(x, source, target):
    spaces = lax.axis_size("space")
    pairs = [(source * spaces + s, target * spaces + s) for s in range(spaces)]
    return lax.ppermute(x, AXES, pairs)


PLANE = (16, 128)
WORK = pltpu.VMEM((3, 3 * DEPTH) + PLANE, jnp.float32)
VMEM_SPEC = pl.BlockSpec(memory_space=pltpu.VMEM)


def call(kernel, name, shapes, inputs, works, units):
    outs = [jax.ShapeDtypeStruct(tuple(shape) + PLANE, jnp.float32) for shape in shapes]
    result = pl.pallas_call(
        kernel,
        name=name,
        out_shape=outs,
        in_specs=[VMEM_SPEC] * len(inputs),
        out_specs=[VMEM_SPEC] * len(outs),
        scratch_shapes=[WORK] * works,
        compiler_params=pltpu.CompilerParams(vmem_limit_bytes=8 << 20),
        cost_estimate=pl.CostEstimate(flops=units * 120000, bytes_accessed=units * 60000, transcendentals=0),
    )(*inputs)
    return result[0] if len(outs) == 1 else result


def emit(kernel, name, inputs, count, before, units):
    specs = [VMEM_SPEC] * len(inputs)
    if before is not None:
        inputs = list(inputs) + [before]
        specs.append(pl.BlockSpec(memory_space=pl.ANY))
    return pl.pallas_call(
        kernel,
        name=name,
        out_shape=jax.ShapeDtypeStruct((16, 3, DEPTH) + PLANE, jnp.float32),
        in_specs=specs,
        out_specs=pl.BlockSpec(memory_space=pl.ANY),
        scratch_shapes=[pltpu.VMEM((count, 3, DEPTH) + PLANE, jnp.float32), WORK, WORK, pltpu.SemaphoreType.DMA((count,))],
        input_output_aliases={} if before is None else {len(inputs) - 1: 0},
        compiler_params=pltpu.CompilerParams(vmem_limit_bytes=8 << 20),
        cost_estimate=pl.CostEstimate(flops=units * 120000, bytes_accessed=units * 60000, transcendentals=0),
    )(*inputs)


def on_device(initial, guesses, viscosity, forcing):
    times = lax.axis_size("tm")
    spaces = lax.axis_size("space")
    column = lax.axis_index("tm")
    every = range(times)
    marcher = times - 1

    incoming = lax.ppermute(
        guesses[3], AXES, [(t * spaces + s, (t + 1) * spaces + s) for t in range(times - 1) for s in range(spaces)]
    )
    opening = jnp.where(column == 0, initial, incoming)
    fields = jnp.concatenate([viscosity[None], forcing], axis=0)
    fields_low, fields_high = halos(fields, fields, every)
    own = guesses[:3]
    guess_low, guess_high = halos(own, own, every)
    open_low, open_high = halos(opening, opening, every)
    initial_low, initial_high = halos(initial, initial, (marcher,))

    table = (5, 3 * DEPTH)
    fine, middle, coarse = call(tables_kernel, "tables", [table] * 3, [fields_low, fields, fields_high], 0, 10)
    defects = call(
        defects_kernel, "defects", [(3, 3, DEPTH)], [guess_low, own, guess_high, fine, middle], 2, 114
    )
    to_up, to_down = call(
        opening_kernel, "opening", [(3, 6)] * 2, [open_low, opening, open_high, fine, defects], 2, 28
    )
    low, high = halos(to_up, to_down, every)
    defect, rest = call(
        remainder_kernel,
        "remainder",
        [(3, DEPTH)] * 2,
        [open_low, opening, open_high, middle, coarse, defects, to_up],
        1,
        20,
    )
    second_up, second_down = call(
        second_kernel, "second", [(3, 8)] * 2, [low, to_up, high, middle, defects, defect, rest], 2, 28
    )
    defect_low, defect_high = halos(second_up, second_down, every)
    term = call(
        coarse_defect_kernel,
        "coarse_defect",
        [(3, 8)],
        [defect_low, second_up, defect_high, middle, rest],
        1,
        18,
    )

    terms = [move(term, t, marcher) for t in range(times - 1)] + [term]
    state, low, high = initial, initial_low, initial_high
    starts = {}
    for period in range(times // 2):
        if period:
            low, high = halos(state, state, (marcher,))
        if 2 * period + 2 < times:
            passed, state = call(
                march_kernel,
                "march",
                [(3, DEPTH)] * 2,
                [low, state, high, coarse, terms[2 * period], terms[2 * period + 1]],
                2,
                28,
            )
            starts[2 * period + 1] = move(passed, marcher, 2 * period + 1)
            starts[2 * period + 2] = move(state, marcher, 2 * period + 2)
        else:
            state = call(last_march_kernel, "last_march", [(3, DEPTH)], [low, state, high, coarse, terms[2 * period]], 1, 10)
    start = jnp.where(column == 0, initial, state)
    for t, arrived in starts.items():
        start = jnp.where(column == t, arrived, start)

    low, high = halos(start, start, every)
    stations = call(
        stations_kernel,
        "stations",
        [(2, 3, DEPTH)],
        [low, start, high, middle, defect_low, defect, defect_high, defects],
        2,
        28,
    )
    station_low, station_high = halos(stations, stations, every)
    result = emit(first_rows_kernel, "first_rows", [low, start, high, fine, coarse, term, stations], 6, None, 28)
    third = call(
        third_kernel, "third", [(3, DEPTH)], [station_low, stations, station_high, middle, defects], 1, 10
    )
    third_low, third_high = halos(third, third, every)
    result = emit(
        middle_rows_kernel, "middle_rows", [station_low, stations, station_high, fine, third], 7, result, 36
    )
    return emit(last_rows_kernel, "last_rows", [third_low, third, third_high, fine], 3, result, 18)


def solution(mesh):
    return jax.shard_map(
        on_device,
        mesh=mesh,
        in_specs=(
            P(None, "space", None, None),
            P("tm", None, "space", None, None),
            P("space", None, None),
            P(None, "space", None, None),
        ),
        out_specs=P("tm", None, "space", None, None),
        check_vma=False,
    )
```

```python
import functools

import jax
import jax.numpy as jnp
from jax import lax
from jax.experimental import pallas as pl
from jax.experimental.pallas import tpu as pltpu
from jax.sharding import PartitionSpec as P

time_step = 0.019
FINE, MIDDLE, COARSE = time_step, 2.0 * time_step, 8.0 * time_step
DEPTH = 4
AXES = ("tm", "space")


GUESSES, INITIAL, FORCING, VISCOSITY = 0, 9, 12, 15


def slab(low, own, high, base=0):
    def get(c, z):
        if z < 0:
            return low[base + c, z + DEPTH]
        if z >= DEPTH:
            return high[base + c, z - DEPTH]
        return own[base + c, z]

    return get


def reader(ref, shift=DEPTH):
    return lambda c, z: ref[c, z + shift]


def writer(ref, shift=DEPTH):
    def put(c, z, value):
        ref[c, z + shift] = value

    return put


def advance(get, put, first, last, table, step_size):
    for z in range(first, last):
        alpha = table[0, z + DEPTH]
        keep = table[1, z + DEPTH]
        center = [get(c, z) for c in range(3)]
        half = [value * (0.5 * step_size) for value in center]
        east, west = alpha - half[0], alpha + half[0]
        north, south = alpha - half[1], alpha + half[1]
        up, down = alpha - half[2], alpha + half[2]
        for c in range(3):
            value = center[c]
            along_x = east * pltpu.roll(value, 127, 1) + west * pltpu.roll(value, 1, 1)
            along_y = north * pltpu.roll(value, 15, 0) + south * pltpu.roll(value, 1, 0)
            along_z = up * get(c, z + 1) + down * get(c, z - 1)
            put(c, z, (keep * value + table[2 + c, z + DEPTH]) + along_x + (along_y + along_z))


def pack_kernel(initial, guesses, viscosity, forcing, last, bulk, sem):
    copies = [pltpu.make_async_copy(guesses.at[3], last, sem.at[0])]
    for i in range(3):
        copies.append(pltpu.make_async_copy(guesses.at[i], bulk.at[pl.ds(3 * i, 3)], sem.at[1 + i]))
    copies.append(pltpu.make_async_copy(initial, bulk.at[pl.ds(INITIAL, 3)], sem.at[4]))
    copies.append(pltpu.make_async_copy(forcing, bulk.at[pl.ds(FORCING, 3)], sem.at[5]))
    copies.append(pltpu.make_async_copy(viscosity, bulk.at[VISCOSITY], sem.at[6]))
    for copy in copies:
        copy.start()
    for copy in copies:
        copy.wait()


def tables_kernel(low, own, high, fine, middle, coarse):
    get = slab(low, own, high, FORCING)
    for table, step_size in ((fine, FINE), (middle, MIDDLE), (coarse, COARSE)):
        for z in range(-DEPTH, 2 * DEPTH):
            alpha = get(3, z) * step_size
            table[0, z + DEPTH] = alpha
            table[1, z + DEPTH] = 1.0 - 6.0 * alpha
            for c in range(3):
                table[2 + c, z + DEPTH] = get(c, z) * step_size


def defects_kernel(low, own, high, fine, middle, out, one, two):
    def body(i, carry):
        start = slab(low, own, high, 3 * i)
        advance(start, writer(one), -3, 7, fine, FINE)
        advance(reader(one), writer(two), -2, 6, fine, FINE)
        advance(reader(two), writer(one), -1, 5, fine, FINE)

        def store(c, z, value):
            out[i, c, z] = value

        def subtract(c, z, value):
            out[i, c, z] = out[i, c, z] - value

        advance(reader(one), store, 0, 4, fine, FINE)
        advance(start, writer(two), -1, 5, middle, MIDDLE)
        advance(reader(two), subtract, 0, 4, middle, MIDDLE)
        return carry

    lax.fori_loop(0, 3, body, 0)


def opening_kernel(low, own, high, fine, defects, to_up, to_down, one, two):
    advance(slab(low, own, high), writer(one), -3, 7, fine, FINE)
    advance(reader(one), writer(two), -2, 6, fine, FINE)
    advance(reader(two), writer(one), -1, 5, fine, FINE)

    def store(c, z, value):
        to_up[c, z] = value
        to_down[c, z] = value

    advance(reader(one), store, 0, 4, fine, FINE)
    for c in range(3):
        for z in range(2):
            to_up[c, 4 + z] = defects[0, c, 2 + z]
            to_down[c, 4 + z] = defects[0, c, z]


def remainder_kernel(low, own, high, middle, coarse, defects, first, defect, rest, one):
    start = slab(low, own, high)
    advance(start, writer(one), -1, 5, middle, MIDDLE)

    def subtract(c, z, value):
        defect[c, z] = first[c, z] - value

    advance(reader(one), subtract, 0, 4, middle, MIDDLE)
    advance(start, writer(one), -1, 5, coarse, COARSE)

    def subtract_rest(c, z, value):
        rest[c, z] = defects[2, c, z] - value

    advance(reader(one), subtract_rest, 0, 4, coarse, COARSE)


def second_kernel(low, own, high, middle, defects, defect, rest, to_up, to_down, one, two):
    def added(c, z, value):
        if z < 0:
            term = low[c, 4 + 2 + z]
        elif z >= DEPTH:
            term = high[c, 4 + z - DEPTH]
        else:
            term = defects[0, c, z]
        two[c, z + DEPTH] = value + term

    def third(c, z, value):
        value = value + defects[1, c, z]
        to_up[c, z] = value
        to_down[c, z] = value

    advance(slab(low, own, high), writer(one), -3, 7, middle, MIDDLE)
    advance(reader(one), added, -2, 6, middle, MIDDLE)
    advance(reader(two), writer(one), -1, 5, middle, MIDDLE)
    advance(reader(one), third, 0, 4, middle, MIDDLE)
    for c in range(3):
        for z in range(2):
            to_up[c, 4 + z] = rest[c, 2 + z]
            to_down[c, 4 + z] = rest[c, z]
            to_up[c, 6 + z] = defect[c, 2 + z]
            to_down[c, 6 + z] = defect[c, z]


def coarse_defect_kernel(low, own, high, middle, rest, out, one):
    def added(c, z, value):
        if z < 0:
            term = low[c, 4 + 2 + z]
        elif z >= DEPTH:
            term = high[c, 4 + z - DEPTH]
        else:
            term = rest[c, z]
        out[c, z + 2] = value + term

    advance(slab(low, own, high), writer(one), -3, 7, middle, MIDDLE)
    advance(reader(one), added, -2, 6, middle, MIDDLE)


def march_kernel(base, flag, low, own, high, coarse, term_one, term_two, term, state, message, one, two):
    marching = flag[0] == 1

    def first(c, z, value):
        value = value + term_one[c, z + 2]
        two[c, z + DEPTH] = value
        if 0 <= z < DEPTH:
            message[c, z] = jnp.where(marching, value, term[c, z])

    def second(c, z, value):
        value = value + term_two[c, z + 2]
        state[c, z] = value
        message[c, z + DEPTH] = jnp.where(marching, value, term[c, z + DEPTH])

    advance(slab(low, own, high, base), writer(one), -3, 7, coarse, COARSE)
    advance(reader(one), first, -2, 6, coarse, COARSE)
    advance(reader(two), writer(one), -1, 5, coarse, COARSE)
    advance(reader(one), second, 0, 4, coarse, COARSE)


def last_march_kernel(low, own, high, coarse, term_one, out_one, one):
    def first(c, z, value):
        out_one[c, z] = value + term_one[c, z + 2]

    advance(slab(low, own, high), writer(one), -1, 5, coarse, COARSE)
    advance(reader(one), first, 0, 4, coarse, COARSE)


def stations_kernel(low, own, high, middle, defect_low, defect, defect_high, defects, out, one, two):
    def first(c, z, value):
        if z < 0:
            term = defect_low[c, 6 + 2 + z]
        elif z >= DEPTH:
            term = defect_high[c, 6 + z - DEPTH]
        else:
            term = defect[c, z]
        value = value + term
        two[c, z + DEPTH] = value
        if 0 <= z < DEPTH:
            out[c, z] = value

    def second(c, z, value):
        out[3 + c, z] = value + defects[0, c, z]

    advance(slab(low, own, high), writer(one), -3, 7, middle, MIDDLE)
    advance(reader(one), first, -2, 6, middle, MIDDLE)
    advance(reader(two), writer(one), -1, 5, middle, MIDDLE)
    advance(reader(one), second, 0, 4, middle, MIDDLE)


def third_kernel(low, own, high, middle, defects, out, one):
    def third(c, z, value):
        out[c, z] = value + defects[1, c, z]

    advance(slab(low, own, high, 3), writer(one), -1, 5, middle, MIDDLE)
    advance(reader(one), third, 0, 4, middle, MIDDLE)


def fine_rows(start, fine, rows, at, one, two):
    def first(c, z, value):
        one[c, z + DEPTH] = value
        if 0 <= z < DEPTH:
            rows[at, c, z] = value

    def second(c, z, value):
        two[c, z + DEPTH] = value
        if 0 <= z < DEPTH:
            rows[at + 1, c, z] = value

    def third(c, z, value):
        rows[at + 2, c, z] = value

    advance(start, first, -2, 6, fine, FINE)
    advance(reader(one), second, -1, 5, fine, FINE)
    advance(reader(two), third, 0, 4, fine, FINE)


def send_rows(rows, result, sem, places):
    copies = [
        pltpu.make_async_copy(rows.at[at], result.at[place], sem.at[at])
        for at, place in enumerate(places)
    ]
    for copy in copies:
        copy.start()
    for copy in copies:
        copy.wait()


def first_rows_kernel(low, own, high, fine, coarse, term, stations, result, rows, one, two, sem):
    start = slab(low, own, high)
    fine_rows(start, fine, rows, 0, one, two)
    for c in range(3):
        for z in range(DEPTH):
            rows[3, c, z] = stations[c, z]
            rows[4, c, z] = stations[3 + c, z]

    def end(c, z, value):
        rows[5, c, z] = value + term[c, z + 2]

    advance(start, writer(one), -1, 5, coarse, COARSE)
    advance(reader(one), end, 0, 4, coarse, COARSE)
    send_rows(rows, result, sem, (0, 1, 2, 3, 7, 15))


def middle_rows_kernel(low, own, high, fine, station, before, result, rows, one, two, sem):
    for i in range(2):
        fine_rows(slab(low, own, high, 3 * i), fine, rows, 3 * i, one, two)
    for c in range(3):
        for z in range(DEPTH):
            rows[6, c, z] = station[c, z]
    send_rows(rows, result, sem, (4, 5, 6, 8, 9, 10, 11))


def last_rows_kernel(low, own, high, fine, before, result, rows, one, two, sem):
    fine_rows(slab(low, own, high), fine, rows, 0, one, two)
    send_rows(rows, result, sem, (12, 13, 14))


def permute(x, moves):
    spaces = lax.axis_size("space")
    times = lax.axis_size("tm")
    pairs = []
    for t in range(times):
        target, by = moves.get(t, (t, 0))
        pairs += [(t * spaces + s, target * spaces + (s + by) % spaces) for s in range(spaces)]
    return lax.ppermute(x, AXES, pairs)


def halos(to_up, to_down, columns):
    return (
        permute(to_up, {t: (t, 1) for t in columns}),
        permute(to_down, {t: (t, -1) for t in columns}),
    )


def cycle(x, *columns):
    return permute(x, {t: (after, 0) for t, after in zip(columns, columns[1:] + columns[:1])})


PLANE = (16, 128)
WORK = pltpu.VMEM((3, 3 * DEPTH) + PLANE, jnp.float32)
VMEM_SPEC = pl.BlockSpec(memory_space=pltpu.VMEM)


def call(kernel, name, shapes, inputs, works, units, flag=False):
    outs = [jax.ShapeDtypeStruct(tuple(shape) + PLANE, jnp.float32) for shape in shapes]
    result = pl.pallas_call(
        kernel,
        name=name,
        out_shape=outs,
        in_specs=[pl.BlockSpec(memory_space=pltpu.SMEM)] * flag + [VMEM_SPEC] * (len(inputs) - flag),
        out_specs=[VMEM_SPEC] * len(outs),
        scratch_shapes=[WORK] * works,
        compiler_params=pltpu.CompilerParams(vmem_limit_bytes=8 << 20),
        cost_estimate=pl.CostEstimate(flops=units * 120000, bytes_accessed=units * 60000, transcendentals=0),
    )(*inputs)
    return result[0] if len(outs) == 1 else result


def emit(kernel, name, inputs, count, before, units):
    specs = [VMEM_SPEC] * len(inputs)
    if before is not None:
        inputs = list(inputs) + [before]
        specs.append(pl.BlockSpec(memory_space=pl.ANY))
    return pl.pallas_call(
        kernel,
        name=name,
        out_shape=jax.ShapeDtypeStruct((16, 3, DEPTH) + PLANE, jnp.float32),
        in_specs=specs,
        out_specs=pl.BlockSpec(memory_space=pl.ANY),
        scratch_shapes=[pltpu.VMEM((count, 3, DEPTH) + PLANE, jnp.float32), WORK, WORK, pltpu.SemaphoreType.DMA((count,))],
        input_output_aliases={} if before is None else {len(inputs) - 1: 0},
        compiler_params=pltpu.CompilerParams(vmem_limit_bytes=8 << 20),
        cost_estimate=pl.CostEstimate(flops=units * 120000, bytes_accessed=units * 60000, transcendentals=0),
    )(*inputs)


def pack(initial, guesses, viscosity, forcing):
    return pl.pallas_call(
        pack_kernel,
        name="pack",
        out_shape=[
            jax.ShapeDtypeStruct((3, DEPTH) + PLANE, jnp.float32),
            jax.ShapeDtypeStruct((16, DEPTH) + PLANE, jnp.float32),
        ],
        in_specs=[pl.BlockSpec(memory_space=pltpu.HBM)] * 4,
        out_specs=[VMEM_SPEC] * 2,
        scratch_shapes=[pltpu.SemaphoreType.DMA((7,))],
        compiler_params=pltpu.CompilerParams(vmem_limit_bytes=8 << 20),
    )(initial, guesses, viscosity, forcing)


def on_device(initial, guesses, viscosity, forcing):
    times = lax.axis_size("tm")
    column = lax.axis_index("tm")
    every = range(times)
    marcher = times - 1
    alone = (marcher,)

    last, bulk = pack(initial, guesses, viscosity, forcing)
    incoming = permute(last, {t: ((t + 1) % times, 0) for t in every})
    bulk_low, bulk_high = halos(bulk, bulk, every)
    opening = jnp.where(column == 0, initial, incoming)
    open_low, open_high = halos(opening, opening, every)

    table = (5, 3 * DEPTH)
    fine, middle, coarse = call(tables_kernel, "tables", [table] * 3, [bulk_low, bulk, bulk_high], 0, 10)
    defects = call(defects_kernel, "defects", [(3, 3, DEPTH)], [bulk_low, bulk, bulk_high, fine, middle], 2, 114)
    to_up, to_down = call(
        opening_kernel, "opening", [(3, 6)] * 2, [open_low, opening, open_high, fine, defects], 2, 28
    )
    low, high = halos(to_up, to_down, every)
    defect, rest = call(
        remainder_kernel,
        "remainder",
        [(3, DEPTH)] * 2,
        [open_low, opening, open_high, middle, coarse, defects, to_up],
        1,
        20,
    )
    second_up, second_down = call(
        second_kernel, "second", [(3, 8)] * 2, [low, to_up, high, middle, defects, defect, rest], 2, 28
    )
    defect_low, defect_high = halos(second_up, second_down, every)
    term = call(
        coarse_defect_kernel,
        "coarse_defect",
        [(3, 8)],
        [defect_low, second_up, defect_high, middle, rest],
        1,
        18,
    )

    flag = (column == marcher).astype(jnp.int32).reshape(1)
    terms = {marcher: term}
    for t in range(min(4, marcher)):
        terms[t] = cycle(term, t, marcher)
    state, low, high, base = bulk, bulk_low, bulk_high, INITIAL
    starts = {}
    message = None
    for period in range(times // 2):
        if period:
            low, high = halos(state, state, alone)
            base = 0
            for i in range(2):
                t = 2 * period + 2 + i
                done = 2 * period - 1 + i
                if t < marcher:
                    terms[t] = starts[done] = cycle(message, t, marcher, done)
                else:
                    starts[done] = cycle(message, marcher, done)
        if 2 * period + 2 < times:
            state, message = call(
                functools.partial(march_kernel, base),
                "march",
                [(3, DEPTH), (3, 8)],
                [flag, low, state, high, coarse, terms[2 * period], terms[2 * period + 1], term],
                2,
                28,
                True,
            )
        else:
            state = call(last_march_kernel, "last_march", [(3, DEPTH)], [low, state, high, coarse, terms[2 * period]], 1, 10)
    start = jnp.where(column == 0, initial, state)
    for t, arrived in starts.items():
        half = arrived[:, :DEPTH] if t % 2 else arrived[:, DEPTH:]
        start = jnp.where(column == t, half, start)

    low, high = halos(start, start, every)
    stations = call(
        stations_kernel,
        "stations",
        [(6, DEPTH)],
        [low, start, high, middle, defect_low, defect, defect_high, defects],
        2,
        28,
    )
    station_low, station_high = halos(stations, stations, every)
    result = emit(first_rows_kernel, "first_rows", [low, start, high, fine, coarse, term, stations], 6, None, 28)
    third = call(
        third_kernel, "third", [(3, DEPTH)], [station_low, stations, station_high, middle, defects], 1, 10
    )
    third_low, third_high = halos(third, third, every)
    result = emit(
        middle_rows_kernel, "middle_rows", [station_low, stations, station_high, fine, third], 7, result, 36
    )
    return emit(last_rows_kernel, "last_rows", [third_low, third, third_high, fine], 3, result, 18)


def solution(mesh):
    return jax.shard_map(
        on_device,
        mesh=mesh,
        in_specs=(
            P(None, "space", None, None),
            P("tm", None, "space", None, None),
            P("space", None, None),
            P(None, "space", None, None),
        ),
        out_specs=P("tm", None, "space", None, None),
        check_vma=False,
    )
```

```python
import functools

import jax
import jax.numpy as jnp
from jax import lax
from jax.experimental import pallas as pl
from jax.experimental.pallas import tpu as pltpu
from jax.sharding import PartitionSpec as P

time_step = 0.019
FINE, MIDDLE, COARSE = time_step, 2.0 * time_step, 8.0 * time_step
DEPTH = 4
AXES = ("tm", "space")


GUESSES, INITIAL, FORCING, VISCOSITY = 0, 9, 12, 15


def slab(low, own, high, base=0):
    def get(c, z):
        if z < 0:
            return low[base + c, z + DEPTH]
        if z >= DEPTH:
            return high[base + c, z - DEPTH]
        return own[base + c, z]

    return get


def reader(ref, shift=DEPTH):
    return lambda c, z: ref[c, z + shift]


def writer(ref, shift=DEPTH):
    def put(c, z, value):
        ref[c, z + shift] = value

    return put


def advance(get, put, first, last, table, step_size):
    for z in range(first, last):
        alpha = table[0, z + DEPTH]
        keep = table[1, z + DEPTH]
        center = [get(c, z) for c in range(3)]
        half = [value * (0.5 * step_size) for value in center]
        east, west = alpha - half[0], alpha + half[0]
        north, south = alpha - half[1], alpha + half[1]
        up, down = alpha - half[2], alpha + half[2]
        for c in range(3):
            value = center[c]
            along_x = east * pltpu.roll(value, 127, 1) + west * pltpu.roll(value, 1, 1)
            along_y = north * pltpu.roll(value, 15, 0) + south * pltpu.roll(value, 1, 0)
            along_z = up * get(c, z + 1) + down * get(c, z - 1)
            put(c, z, (keep * value + table[2 + c, z + DEPTH]) + along_x + (along_y + along_z))


def tables_kernel(low, own, high, fine, middle, coarse):
    get = slab(low, own, high, FORCING)
    for table, step_size in ((fine, FINE), (middle, MIDDLE), (coarse, COARSE)):
        for z in range(-DEPTH, 2 * DEPTH):
            alpha = get(3, z) * step_size
            table[0, z + DEPTH] = alpha
            table[1, z + DEPTH] = 1.0 - 6.0 * alpha
            for c in range(3):
                table[2 + c, z + DEPTH] = get(c, z) * step_size


def defects_kernel(low, own, high, fine, middle, out, one, two):
    def body(i, carry):
        start = slab(low, own, high, 3 * i)
        advance(start, writer(one), -3, 7, fine, FINE)
        advance(reader(one), writer(two), -2, 6, fine, FINE)
        advance(reader(two), writer(one), -1, 5, fine, FINE)

        def store(c, z, value):
            out[i, c, z] = value

        def subtract(c, z, value):
            out[i, c, z] = out[i, c, z] - value

        advance(reader(one), store, 0, 4, fine, FINE)
        advance(start, writer(two), -1, 5, middle, MIDDLE)
        advance(reader(two), subtract, 0, 4, middle, MIDDLE)
        return carry

    lax.fori_loop(0, 3, body, 0)


def opening_kernel(low, own, high, fine, defects, to_up, to_down, one, two):
    advance(slab(low, own, high), writer(one), -3, 7, fine, FINE)
    advance(reader(one), writer(two), -2, 6, fine, FINE)
    advance(reader(two), writer(one), -1, 5, fine, FINE)

    def store(c, z, value):
        to_up[c, z] = value
        to_down[c, z] = value

    advance(reader(one), store, 0, 4, fine, FINE)
    for c in range(3):
        for z in range(2):
            to_up[c, 4 + z] = defects[0, c, 2 + z]
            to_down[c, 4 + z] = defects[0, c, z]


def remainder_kernel(low, own, high, middle, coarse, defects, first, defect, rest, one):
    start = slab(low, own, high)
    advance(start, writer(one), -1, 5, middle, MIDDLE)

    def subtract(c, z, value):
        defect[c, z] = first[c, z] - value

    advance(reader(one), subtract, 0, 4, middle, MIDDLE)
    advance(start, writer(one), -1, 5, coarse, COARSE)

    def subtract_rest(c, z, value):
        rest[c, z] = defects[2, c, z] - value

    advance(reader(one), subtract_rest, 0, 4, coarse, COARSE)


def second_kernel(low, own, high, middle, defects, defect, rest, to_up, to_down, one, two):
    def added(c, z, value):
        if z < 0:
            term = low[c, 4 + 2 + z]
        elif z >= DEPTH:
            term = high[c, 4 + z - DEPTH]
        else:
            term = defects[0, c, z]
        two[c, z + DEPTH] = value + term

    def third(c, z, value):
        value = value + defects[1, c, z]
        to_up[c, z] = value
        to_down[c, z] = value

    advance(slab(low, own, high), writer(one), -3, 7, middle, MIDDLE)
    advance(reader(one), added, -2, 6, middle, MIDDLE)
    advance(reader(two), writer(one), -1, 5, middle, MIDDLE)
    advance(reader(one), third, 0, 4, middle, MIDDLE)
    for c in range(3):
        for z in range(2):
            to_up[c, 4 + z] = rest[c, 2 + z]
            to_down[c, 4 + z] = rest[c, z]
            to_up[c, 6 + z] = defect[c, 2 + z]
            to_down[c, 6 + z] = defect[c, z]


def coarse_defect_kernel(low, own, high, middle, rest, out, one):
    def added(c, z, value):
        if z < 0:
            term = low[c, 4 + 2 + z]
        elif z >= DEPTH:
            term = high[c, 4 + z - DEPTH]
        else:
            term = rest[c, z]
        out[c, z + 2] = value + term

    advance(slab(low, own, high), writer(one), -3, 7, middle, MIDDLE)
    advance(reader(one), added, -2, 6, middle, MIDDLE)


def march_kernel(base, flag, low, own, high, coarse, term_one, term_two, term, state, message, one, two):
    marching = flag[0] == 1

    def first(c, z, value):
        value = value + term_one[c, z + 2]
        two[c, z + DEPTH] = value
        if 0 <= z < DEPTH:
            message[c, z] = jnp.where(marching, value, term[c, z])

    def second(c, z, value):
        value = value + term_two[c, z + 2]
        state[c, z] = value
        message[c, z + DEPTH] = jnp.where(marching, value, term[c, z + DEPTH])

    advance(slab(low, own, high, base), writer(one), -3, 7, coarse, COARSE)
    advance(reader(one), first, -2, 6, coarse, COARSE)
    advance(reader(two), writer(one), -1, 5, coarse, COARSE)
    advance(reader(one), second, 0, 4, coarse, COARSE)


def last_march_kernel(low, own, high, coarse, term_one, out_one, one):
    def first(c, z, value):
        out_one[c, z] = value + term_one[c, z + 2]

    advance(slab(low, own, high), writer(one), -1, 5, coarse, COARSE)
    advance(reader(one), first, 0, 4, coarse, COARSE)


def stations_kernel(low, own, high, middle, defect_low, defect, defect_high, defects, out, one, two):
    def first(c, z, value):
        if z < 0:
            term = defect_low[c, 6 + 2 + z]
        elif z >= DEPTH:
            term = defect_high[c, 6 + z - DEPTH]
        else:
            term = defect[c, z]
        value = value + term
        two[c, z + DEPTH] = value
        if 0 <= z < DEPTH:
            out[c, z] = value

    def second(c, z, value):
        out[3 + c, z] = value + defects[0, c, z]

    advance(slab(low, own, high), writer(one), -3, 7, middle, MIDDLE)
    advance(reader(one), first, -2, 6, middle, MIDDLE)
    advance(reader(two), writer(one), -1, 5, middle, MIDDLE)
    advance(reader(one), second, 0, 4, middle, MIDDLE)


def third_kernel(low, own, high, middle, defects, out, one):
    def third(c, z, value):
        out[c, z] = value + defects[1, c, z]

    advance(slab(low, own, high, 3), writer(one), -1, 5, middle, MIDDLE)
    advance(reader(one), third, 0, 4, middle, MIDDLE)


def fine_rows(start, fine, rows, at, one, two):
    def first(c, z, value):
        one[c, z + DEPTH] = value
        if 0 <= z < DEPTH:
            rows[at, c, z] = value

    def second(c, z, value):
        two[c, z + DEPTH] = value
        if 0 <= z < DEPTH:
            rows[at + 1, c, z] = value

    def third(c, z, value):
        rows[at + 2, c, z] = value

    advance(start, first, -2, 6, fine, FINE)
    advance(reader(one), second, -1, 5, fine, FINE)
    advance(reader(two), third, 0, 4, fine, FINE)


def send_rows(rows, result, sem, places):
    copies = [
        pltpu.make_async_copy(rows.at[at], result.at[place], sem.at[at])
        for at, place in enumerate(places)
    ]
    for copy in copies:
        copy.start()
    for copy in copies:
        copy.wait()


def first_rows_kernel(low, own, high, fine, coarse, term, stations, result, rows, one, two, sem):
    start = slab(low, own, high)
    fine_rows(start, fine, rows, 0, one, two)
    for c in range(3):
        for z in range(DEPTH):
            rows[3, c, z] = stations[c, z]
            rows[4, c, z] = stations[3 + c, z]

    def end(c, z, value):
        rows[5, c, z] = value + term[c, z + 2]

    advance(start, writer(one), -1, 5, coarse, COARSE)
    advance(reader(one), end, 0, 4, coarse, COARSE)
    send_rows(rows, result, sem, (0, 1, 2, 3, 7, 15))


def middle_rows_kernel(low, own, high, fine, station, before, result, rows, one, two, sem):
    for i in range(2):
        fine_rows(slab(low, own, high, 3 * i), fine, rows, 3 * i, one, two)
    for c in range(3):
        for z in range(DEPTH):
            rows[6, c, z] = station[c, z]
    send_rows(rows, result, sem, (4, 5, 6, 8, 9, 10, 11))


def last_rows_kernel(low, own, high, fine, before, result, rows, one, two, sem):
    fine_rows(slab(low, own, high), fine, rows, 0, one, two)
    send_rows(rows, result, sem, (12, 13, 14))


def permute(x, moves):
    spaces = lax.axis_size("space")
    times = lax.axis_size("tm")
    pairs = []
    for t in range(times):
        if t in moves:
            target, by = moves[t]
            pairs += [(t * spaces + s, target * spaces + (s + by) % spaces) for s in range(spaces)]
        else:
            pairs += [(t * spaces + s, t * spaces + (s ^ 1)) for s in range(spaces)]
    return lax.ppermute(x, AXES, pairs)


def halos(to_up, to_down, columns):
    return (
        permute(to_up, {t: (t, 1) for t in columns}),
        permute(to_down, {t: (t, -1) for t in columns}),
    )


def cycle(x, *columns):
    return permute(x, {t: (after, 0) for t, after in zip(columns, columns[1:] + columns[:1])})


PLANE = (16, 128)
WORK = pltpu.VMEM((3, 3 * DEPTH) + PLANE, jnp.float32)
VMEM_SPEC = pl.BlockSpec(memory_space=pltpu.VMEM)


def call(kernel, name, shapes, inputs, works, units, flag=False):
    outs = [jax.ShapeDtypeStruct(tuple(shape) + PLANE, jnp.float32) for shape in shapes]
    result = pl.pallas_call(
        kernel,
        name=name,
        out_shape=outs,
        in_specs=[pl.BlockSpec(memory_space=pltpu.SMEM)] * flag + [VMEM_SPEC] * (len(inputs) - flag),
        out_specs=[VMEM_SPEC] * len(outs),
        scratch_shapes=[WORK] * works,
        compiler_params=pltpu.CompilerParams(vmem_limit_bytes=8 << 20),
        cost_estimate=pl.CostEstimate(flops=units * 120000, bytes_accessed=units * 60000, transcendentals=0),
    )(*inputs)
    return result[0] if len(outs) == 1 else result


def emit(kernel, name, inputs, count, before, units):
    specs = [VMEM_SPEC] * len(inputs)
    if before is not None:
        inputs = list(inputs) + [before]
        specs.append(pl.BlockSpec(memory_space=pl.ANY))
    return pl.pallas_call(
        kernel,
        name=name,
        out_shape=jax.ShapeDtypeStruct((16, 3, DEPTH) + PLANE, jnp.float32),
        in_specs=specs,
        out_specs=pl.BlockSpec(memory_space=pl.ANY),
        scratch_shapes=[pltpu.VMEM((count, 3, DEPTH) + PLANE, jnp.float32), WORK, WORK, pltpu.SemaphoreType.DMA((count,))],
        input_output_aliases={} if before is None else {len(inputs) - 1: 0},
        compiler_params=pltpu.CompilerParams(vmem_limit_bytes=8 << 20),
        cost_estimate=pl.CostEstimate(flops=units * 120000, bytes_accessed=units * 60000, transcendentals=0),
    )(*inputs)


def pack(initial, guesses, viscosity, forcing):
    last, guesses = lax.optimization_barrier((guesses[3], guesses))
    members = guesses[:3].reshape((9,) + guesses.shape[2:])
    return last, jnp.concatenate([members, initial, forcing, viscosity[None]], axis=0)


def on_device(initial, guesses, viscosity, forcing):
    times = lax.axis_size("tm")
    column = lax.axis_index("tm")
    every = range(times)
    marcher = times - 1
    alone = (marcher,)

    last, bulk = pack(initial, guesses, viscosity, forcing)
    incoming = permute(last, {t: ((t + 1) % times, 0) for t in every})
    bulk_low, bulk_high = halos(bulk, bulk, every)
    opening = jnp.where(column == 0, initial, incoming)
    open_low, open_high = halos(opening, opening, every)

    table = (5, 3 * DEPTH)
    fine, middle, coarse = call(tables_kernel, "tables", [table] * 3, [bulk_low, bulk, bulk_high], 0, 10)
    defects = call(defects_kernel, "defects", [(3, 3, DEPTH)], [bulk_low, bulk, bulk_high, fine, middle], 2, 114)
    to_up, to_down = call(
        opening_kernel, "opening", [(3, 6)] * 2, [open_low, opening, open_high, fine, defects], 2, 28
    )
    low, high = halos(to_up, to_down, every)
    defect, rest = call(
        remainder_kernel,
        "remainder",
        [(3, DEPTH)] * 2,
        [open_low, opening, open_high, middle, coarse, defects, to_up],
        1,
        20,
    )
    second_up, second_down = call(
        second_kernel, "second", [(3, 8)] * 2, [low, to_up, high, middle, defects, defect, rest], 2, 28
    )
    defect_low, defect_high = halos(second_up, second_down, every)
    term = call(
        coarse_defect_kernel,
        "coarse_defect",
        [(3, 8)],
        [defect_low, second_up, defect_high, middle, rest],
        1,
        18,
    )

    flag = (column == marcher).astype(jnp.int32).reshape(1)
    terms = {marcher: term}
    for t in range(min(4, marcher)):
        terms[t] = cycle(term, t, marcher)
    state, low, high, base = bulk, bulk_low, bulk_high, INITIAL
    starts = {}
    message = None
    for period in range(times // 2):
        if period:
            low, high = halos(state, state, alone)
            base = 0
            for i in range(2):
                t = 2 * period + 2 + i
                done = 2 * period - 1 + i
                if t < marcher:
                    terms[t] = starts[done] = cycle(message, t, marcher, done)
                else:
                    starts[done] = cycle(message, marcher, done)
        if 2 * period + 2 < times:
            state, message = call(
                functools.partial(march_kernel, base),
                "march",
                [(3, DEPTH), (3, 8)],
                [flag, low, state, high, coarse, terms[2 * period], terms[2 * period + 1], term],
                2,
                28,
                True,
            )
        else:
            state = call(last_march_kernel, "last_march", [(3, DEPTH)], [low, state, high, coarse, terms[2 * period]], 1, 10)
    start = jnp.where(column == 0, initial, state)
    for t, arrived in starts.items():
        half = arrived[:, :DEPTH] if t % 2 else arrived[:, DEPTH:]
        start = jnp.where(column == t, half, start)

    low, high = halos(start, start, every)
    stations = call(
        stations_kernel,
        "stations",
        [(6, DEPTH)],
        [low, start, high, middle, defect_low, defect, defect_high, defects],
        2,
        28,
    )
    station_low, station_high = halos(stations, stations, every)
    result = emit(first_rows_kernel, "first_rows", [low, start, high, fine, coarse, term, stations], 6, None, 28)
    third = call(
        third_kernel, "third", [(3, DEPTH)], [station_low, stations, station_high, middle, defects], 1, 10
    )
    third_low, third_high = halos(third, third, every)
    result = emit(
        middle_rows_kernel, "middle_rows", [station_low, stations, station_high, fine, third], 7, result, 36
    )
    return emit(last_rows_kernel, "last_rows", [third_low, third, third_high, fine], 3, result, 18)


def solution(mesh):
    return jax.shard_map(
        on_device,
        mesh=mesh,
        in_specs=(
            P(None, "space", None, None),
            P("tm", None, "space", None, None),
            P("space", None, None),
            P(None, "space", None, None),
        ),
        out_specs=P("tm", None, "space", None, None),
        check_vma=False,
    )
```

```python
import functools

import jax
import jax.numpy as jnp
from jax import lax
from jax.experimental import pallas as pl
from jax.experimental.pallas import tpu as pltpu
from jax.sharding import PartitionSpec as P


time_step = 0.019
FINE, MIDDLE, COARSE = time_step, 2.0 * time_step, 8.0 * time_step
DEPTH = 4
AXES = ("tm", "space")


INITIAL, FORCING = 9, 12


def slab(low, own, high, base=0):
    def get(c, z):
        if z < 0:
            return low[base + c, z + DEPTH]
        if z >= DEPTH:
            return high[base + c, z - DEPTH]
        return own[base + c, z]

    return get


def reader(ref, shift=DEPTH):
    return lambda c, z: ref[c, z + shift]


def writer(ref, shift=DEPTH):
    def put(c, z, value):
        ref[c, z + shift] = value

    return put


def advance(get, put, first, last, table, step_size):
    for z in range(first, last):
        alpha = table[0, z + DEPTH]
        keep = table[1, z + DEPTH]
        center = [get(c, z) for c in range(3)]
        half = [value * (0.5 * step_size) for value in center]
        east, west = alpha - half[0], alpha + half[0]
        north, south = alpha - half[1], alpha + half[1]
        up, down = alpha - half[2], alpha + half[2]
        for c in range(3):
            value = center[c]
            along_x = east * pltpu.roll(value, 127, 1) + west * pltpu.roll(value, 1, 1)
            along_y = north * pltpu.roll(value, 15, 0) + south * pltpu.roll(value, 1, 0)
            along_z = up * get(c, z + 1) + down * get(c, z - 1)
            put(c, z, (keep * value + table[2 + c, z + DEPTH]) + along_x + (along_y + along_z))


def tables_kernel(low, own, high, fine, middle, coarse, first_low, first, first_high, kept):
    for source, target in ((low, first_low), (own, first), (high, first_high), (own, kept)):
        for c in range(3):
            for z in range(DEPTH):
                target[c, z] = source[INITIAL + c, z]
    get = slab(low, own, high, FORCING)
    for table, step_size in ((fine, FINE), (middle, MIDDLE), (coarse, COARSE)):
        for z in range(-DEPTH, 2 * DEPTH):
            alpha = get(3, z) * step_size
            table[0, z + DEPTH] = alpha
            table[1, z + DEPTH] = 1.0 - 6.0 * alpha
            for c in range(3):
                table[2 + c, z + DEPTH] = get(c, z) * step_size


def defects_kernel(low, own, high, fine, middle, out, one, two):
    def body(i, carry):
        start = slab(low, own, high, 3 * i)
        advance(start, writer(one), -3, 7, fine, FINE)
        advance(reader(one), writer(two), -2, 6, fine, FINE)
        advance(reader(two), writer(one), -1, 5, fine, FINE)

        def store(c, z, value):
            out[i, c, z] = value

        def subtract(c, z, value):
            out[i, c, z] = out[i, c, z] - value

        advance(reader(one), store, 0, 4, fine, FINE)
        advance(start, writer(two), -1, 5, middle, MIDDLE)
        advance(reader(two), subtract, 0, 4, middle, MIDDLE)
        return carry

    lax.fori_loop(0, 3, body, 0)


def opening_kernel(low, own, high, fine, defects, to_up, to_down, one, two):
    advance(slab(low, own, high), writer(one), -3, 7, fine, FINE)
    advance(reader(one), writer(two), -2, 6, fine, FINE)
    advance(reader(two), writer(one), -1, 5, fine, FINE)

    def store(c, z, value):
        to_up[c, z] = value
        to_down[c, z] = value

    advance(reader(one), store, 0, 4, fine, FINE)
    for c in range(3):
        for z in range(2):
            to_up[c, 4 + z] = defects[0, c, 2 + z]
            to_down[c, 4 + z] = defects[0, c, z]


def remainder_kernel(low, own, high, middle, coarse, defects, first, defect, rest, one):
    start = slab(low, own, high)
    advance(start, writer(one), -1, 5, middle, MIDDLE)

    def subtract(c, z, value):
        defect[c, z] = first[c, z] - value

    advance(reader(one), subtract, 0, 4, middle, MIDDLE)
    advance(start, writer(one), -1, 5, coarse, COARSE)

    def subtract_rest(c, z, value):
        rest[c, z] = defects[2, c, z] - value

    advance(reader(one), subtract_rest, 0, 4, coarse, COARSE)


def second_kernel(low, own, high, middle, defects, defect, rest, to_up, to_down, one, two):
    def added(c, z, value):
        if z < 0:
            term = low[c, 4 + 2 + z]
        elif z >= DEPTH:
            term = high[c, 4 + z - DEPTH]
        else:
            term = defects[0, c, z]
        two[c, z + DEPTH] = value + term

    def third(c, z, value):
        value = value + defects[1, c, z]
        to_up[c, z] = value
        to_down[c, z] = value

    advance(slab(low, own, high), writer(one), -3, 7, middle, MIDDLE)
    advance(reader(one), added, -2, 6, middle, MIDDLE)
    advance(reader(two), writer(one), -1, 5, middle, MIDDLE)
    advance(reader(one), third, 0, 4, middle, MIDDLE)
    for c in range(3):
        for z in range(2):
            to_up[c, 4 + z] = rest[c, 2 + z]
            to_down[c, 4 + z] = rest[c, z]
            to_up[c, 6 + z] = defect[c, 2 + z]
            to_down[c, 6 + z] = defect[c, z]


def coarse_defect_kernel(low, own, high, middle, rest, out, middle_out, one):
    def added(c, z, value):
        if z < 0:
            term = low[c, 4 + 2 + z]
        elif z >= DEPTH:
            term = high[c, 4 + z - DEPTH]
        else:
            term = rest[c, z]
        out[c, z + 2] = value + term
        if 0 <= z < DEPTH:
            middle_out[c, z] = value + term

    advance(slab(low, own, high), writer(one), -3, 7, middle, MIDDLE)
    advance(reader(one), added, -2, 6, middle, MIDDLE)


def take(kept, arrived, shift):
    for c in range(3):
        for z in range(DEPTH):
            kept[c, z] = arrived[c, z + shift]


def march_kernel(
    done, low, own, high, coarse, term_one, term_two, term, kept_in,
    state, message_one, message_two, kept, one, two,
):
    def first(c, z, value):
        value = value + term_one[c, z + 2]
        two[c, z + DEPTH] = value
        message_one[c, z + 2] = value

    def second(c, z, value):
        value = value + term_two[c, z]
        state[c, z] = value
        message_two[c, z] = value

    column = lax.axis_index("tm")
    marching = column == lax.axis_size("tm") - 1

    @pl.when(marching)
    def _():
        advance(slab(low, own, high), writer(one), -3, 7, coarse, COARSE)
        advance(reader(one), first, -2, 6, coarse, COARSE)
        advance(reader(two), writer(one), -1, 5, coarse, COARSE)
        advance(reader(one), second, 0, 4, coarse, COARSE)

    @pl.when(jnp.logical_not(marching))
    def _():
        for c in range(3):
            for z in range(2 * DEPTH):
                message_one[c, z] = term[c, z]
            for z in range(DEPTH):
                message_two[c, z] = term[c, z + 2]
                state[c, z] = own[c, z]

    if done[0] is not None:
        pl.when(column == done[0])(functools.partial(take, kept, term_one, 2))
    if done[1] is not None:
        pl.when(column == done[1])(functools.partial(take, kept, term_two, 0))


def last_march_kernel(done, low, own, high, coarse, term_one, kept, *rest):
    arrivals, (start, one) = rest[:-2], rest[-2:]
    column = lax.axis_index("tm")
    marching = column == lax.axis_size("tm") - 1

    def first(c, z, value):
        start[c, z] = value + term_one[c, z + 2]

    @pl.when(marching)
    def _():
        advance(slab(low, own, high), writer(one), -1, 5, coarse, COARSE)
        advance(reader(one), first, 0, 4, coarse, COARSE)

    pl.when(jnp.logical_not(marching))(functools.partial(take, start, kept, 0))
    for t, arrived in zip(done, (term_one,) + arrivals):
        if t is not None:
            pl.when(column == t)(functools.partial(take, start, arrived, 2 if t % 2 else 0))


def stations_kernel(low, own, high, middle, defect_low, defect, defect_high, defects, out, one, two):
    def first(c, z, value):
        if z < 0:
            term = defect_low[c, 6 + 2 + z]
        elif z >= DEPTH:
            term = defect_high[c, 6 + z - DEPTH]
        else:
            term = defect[c, z]
        value = value + term
        two[c, z + DEPTH] = value
        if 0 <= z < DEPTH:
            out[c, z] = value

    def second(c, z, value):
        out[3 + c, z] = value + defects[0, c, z]

    advance(slab(low, own, high), writer(one), -3, 7, middle, MIDDLE)
    advance(reader(one), first, -2, 6, middle, MIDDLE)
    advance(reader(two), writer(one), -1, 5, middle, MIDDLE)
    advance(reader(one), second, 0, 4, middle, MIDDLE)


def third_kernel(low, own, high, middle, defects, out, one):
    def third(c, z, value):
        out[c, z] = value + defects[1, c, z]

    advance(slab(low, own, high, 3), writer(one), -1, 5, middle, MIDDLE)
    advance(reader(one), third, 0, 4, middle, MIDDLE)


def fine_rows(start, fine, rows, at, one, two):
    def first(c, z, value):
        one[c, z + DEPTH] = value
        if 0 <= z < DEPTH:
            rows[at, c, z] = value

    def second(c, z, value):
        two[c, z + DEPTH] = value
        if 0 <= z < DEPTH:
            rows[at + 1, c, z] = value

    def third(c, z, value):
        rows[at + 2, c, z] = value

    advance(start, first, -2, 6, fine, FINE)
    advance(reader(one), second, -1, 5, fine, FINE)
    advance(reader(two), third, 0, 4, fine, FINE)


def send_rows(rows, result, sem, places):
    copies = [
        pltpu.make_async_copy(rows.at[at], result.at[place], sem.at[at])
        for at, place in enumerate(places)
    ]
    for copy in copies:
        copy.start()
    for copy in copies:
        copy.wait()


def first_rows_kernel(low, own, high, fine, coarse, term, stations, result, rows, one, two, sem):
    start = slab(low, own, high)
    fine_rows(start, fine, rows, 0, one, two)
    for c in range(3):
        for z in range(DEPTH):
            rows[3, c, z] = stations[c, z]
            rows[4, c, z] = stations[3 + c, z]

    def end(c, z, value):
        rows[5, c, z] = value + term[c, z + 2]

    advance(start, writer(one), -1, 5, coarse, COARSE)
    advance(reader(one), end, 0, 4, coarse, COARSE)
    send_rows(rows, result, sem, (0, 1, 2, 3, 7, 15))


def middle_rows_kernel(low, own, high, fine, station, before, result, rows, one, two, sem):
    for i in range(2):
        fine_rows(slab(low, own, high, 3 * i), fine, rows, 3 * i, one, two)
    for c in range(3):
        for z in range(DEPTH):
            rows[6, c, z] = station[c, z]
    send_rows(rows, result, sem, (4, 5, 6, 8, 9, 10, 11))


def last_rows_kernel(low, own, high, fine, before, result, rows, one, two, sem):
    fine_rows(slab(low, own, high), fine, rows, 0, one, two)
    send_rows(rows, result, sem, (12, 13, 14))


def permute(x, moves):
    spaces = lax.axis_size("space")
    times = lax.axis_size("tm")
    pairs = []
    for t in range(times):
        if t in moves:
            target, by = moves[t]
            pairs += [(t * spaces + s, target * spaces + (s + by) % spaces) for s in range(spaces)]
        else:
            pairs += [(t * spaces + s, t * spaces + (s ^ 1)) for s in range(spaces)]
    return lax.ppermute(x, AXES, pairs)


def halos(to_up, to_down, columns):
    return (
        permute(to_up, {t: (t, 1) for t in columns}),
        permute(to_down, {t: (t, -1) for t in columns}),
    )


def cycle(x, *columns):
    return permute(x, {t: (after, 0) for t, after in zip(columns, columns[1:] + columns[:1])})


PLANE = (16, 128)
WORK = pltpu.VMEM((3, 3 * DEPTH) + PLANE, jnp.float32)
VMEM_SPEC = pl.BlockSpec(memory_space=pltpu.VMEM)


def call(kernel, shapes, inputs, works, units, aliases=None):
    outs = [jax.ShapeDtypeStruct(tuple(shape) + PLANE, jnp.float32) for shape in shapes]
    result = pl.pallas_call(
        kernel,
        out_shape=outs,
        in_specs=[VMEM_SPEC] * len(inputs),
        out_specs=[VMEM_SPEC] * len(outs),
        scratch_shapes=[WORK] * works,
        input_output_aliases=aliases or {},
        compiler_params=pltpu.CompilerParams(vmem_limit_bytes=8 << 20),
        cost_estimate=pl.CostEstimate(flops=units * 120000, bytes_accessed=units * 60000, transcendentals=0),
    )(*inputs)
    return result[0] if len(outs) == 1 else result


def emit(kernel, inputs, count, before, units):
    specs = [VMEM_SPEC] * len(inputs)
    if before is not None:
        inputs = list(inputs) + [before]
        specs.append(pl.BlockSpec(memory_space=pl.ANY))
    return pl.pallas_call(
        kernel,
        out_shape=jax.ShapeDtypeStruct((16, 3, DEPTH) + PLANE, jnp.float32),
        in_specs=specs,
        out_specs=pl.BlockSpec(memory_space=pl.ANY),
        scratch_shapes=[pltpu.VMEM((count, 3, DEPTH) + PLANE, jnp.float32), WORK, WORK, pltpu.SemaphoreType.DMA((count,))],
        input_output_aliases={} if before is None else {len(inputs) - 1: 0},
        compiler_params=pltpu.CompilerParams(vmem_limit_bytes=8 << 20),
        cost_estimate=pl.CostEstimate(flops=units * 120000, bytes_accessed=units * 60000, transcendentals=0),
    )(*inputs)


def pack(initial, guesses, viscosity, forcing):
    last, guesses = lax.optimization_barrier((guesses[3], guesses))
    members = guesses[:3].reshape((9,) + guesses.shape[2:])
    return last, jnp.concatenate([members, initial, forcing, viscosity[None]], axis=0)


def on_device(initial, guesses, viscosity, forcing):
    times = lax.axis_size("tm")
    column = lax.axis_index("tm")
    every = range(times)
    marcher = times - 1
    alone = (marcher,)

    last, bulk = pack(initial, guesses, viscosity, forcing)
    incoming = permute(last, {t: ((t + 1) % times, 0) for t in every})
    bulk_low, bulk_high = halos(bulk, bulk, every)
    opening = jnp.where(column == 0, bulk[INITIAL : INITIAL + 3], incoming)
    open_low, open_high = halos(opening, opening, every)

    table = (5, 3 * DEPTH)
    fine, middle, coarse, first_low, first, first_high, kept = call(
        tables_kernel, [table] * 3 + [(3, DEPTH)] * 4, [bulk_low, bulk, bulk_high], 0, 10
    )
    defects = call(defects_kernel, [(3, 3, DEPTH)], [bulk_low, bulk, bulk_high, fine, middle], 2, 114)
    to_up, to_down = call(opening_kernel, [(3, 6)] * 2, [open_low, opening, open_high, fine, defects], 2, 28)
    low, high = halos(to_up, to_down, every)
    defect, rest = call(
        remainder_kernel, [(3, DEPTH)] * 2, [open_low, opening, open_high, middle, coarse, defects, to_up], 1, 20
    )
    second_up, second_down = call(second_kernel, [(3, 8)] * 2, [low, to_up, high, middle, defects, defect, rest], 2, 28)
    defect_low, defect_high = halos(second_up, second_down, every)
    term, term_middle = call(
        coarse_defect_kernel, [(3, 8), (3, DEPTH)], [defect_low, second_up, defect_high, middle, rest], 1, 18
    )

    terms = {marcher: term}
    ahead = (term, term_middle)
    for t in range(min(6, marcher)):
        terms[t] = cycle(ahead[t % 2], t, marcher)
        if t % 2:
            ahead = lax.optimization_barrier((term, term_middle, terms[t - 1], terms[t]))
            ahead, (terms[t - 1], terms[t]) = ahead[:2], ahead[2:]
    state, low, high = first, first_low, first_high
    brought, extra = {}, {}
    messages = None
    for period in range(times // 2):
        if period:
            low, high = halos(state, state, alone)
            for i in range(2):
                t = 2 * period + 4 + i
                done = 2 * period - 1 + i
                if t < marcher:
                    terms[t] = cycle(messages[i], t, marcher, done)
                    brought[t] = done
                else:
                    extra[done] = cycle(messages[i], marcher, done)
        if 2 * period + 2 < times:
            pair = (2 * period, 2 * period + 1)
            state, *messages, kept = call(
                functools.partial(march_kernel, [brought.get(t) for t in pair]),
                [(3, DEPTH), (3, 8), (3, DEPTH), (3, DEPTH)],
                [low, state, high, coarse, terms[pair[0]], terms[pair[1]], term, kept],
                2,
                28,
                {7: 3},
            )
        else:
            start = call(
                functools.partial(last_march_kernel, [brought.get(2 * period)] + list(extra)),
                [(3, DEPTH)],
                [low, state, high, coarse, terms[2 * period], kept] + list(extra.values()),
                1,
                10,
            )

    low, high = halos(start, start, every)
    stations = call(
        stations_kernel, [(6, DEPTH)], [low, start, high, middle, defect_low, defect, defect_high, defects], 2, 28
    )
    station_low, station_high = halos(stations, stations, every)
    result = emit(first_rows_kernel, [low, start, high, fine, coarse, term, stations], 6, None, 28)
    third = call(third_kernel, [(3, DEPTH)], [station_low, stations, station_high, middle, defects], 1, 10)
    third_low, third_high = halos(third, third, every)
    result = emit(middle_rows_kernel, [station_low, stations, station_high, fine, third], 7, result, 36)
    return emit(last_rows_kernel, [third_low, third, third_high, fine], 3, result, 18)


def solution(mesh):
    return jax.shard_map(
        on_device,
        mesh=mesh,
        in_specs=(
            P(None, "space", None, None),
            P("tm", None, "space", None, None),
            P("space", None, None),
            P(None, "space", None, None),
        ),
        out_specs=P("tm", None, "space", None, None),
        check_vma=False,
    )
```

```python
import functools

import jax
import jax.numpy as jnp
from jax import lax
from jax.experimental import pallas as pl
from jax.experimental.pallas import tpu as pltpu
from jax.sharding import PartitionSpec as P


time_step = 0.019
FINE, MIDDLE, COARSE = time_step, 2.0 * time_step, 8.0 * time_step
DEPTH = 4
AXES = ("tm", "space")


def slab(low, own, high, base=0):
    def get(c, z):
        if z < 0:
            return low[base + c, z + DEPTH]
        if z >= DEPTH:
            return high[base + c, z - DEPTH]
        return own[base + c, z]

    return get


def reader(ref, shift=DEPTH):
    return lambda c, z: ref[c, z + shift]


def writer(ref, shift=DEPTH):
    def put(c, z, value):
        ref[c, z + shift] = value

    return put


def advance(get, put, first, last, table, step_size):
    for z in range(first, last):
        alpha = table[0, z + DEPTH]
        keep = table[1, z + DEPTH]
        center = [get(c, z) for c in range(3)]
        half = [value * (0.5 * step_size) for value in center]
        east, west = alpha - half[0], alpha + half[0]
        north, south = alpha - half[1], alpha + half[1]
        up, down = alpha - half[2], alpha + half[2]
        for c in range(3):
            value = center[c]
            along_x = east * pltpu.roll(value, 127, 1) + west * pltpu.roll(value, 1, 1)
            along_y = north * pltpu.roll(value, 15, 0) + south * pltpu.roll(value, 1, 0)
            along_z = up * get(c, z + 1) + down * get(c, z - 1)
            put(c, z, (keep * value + table[2 + c, z + DEPTH]) + along_x + (along_y + along_z))


def tables_kernel(low, own, high, fine, middle, coarse):
    get = slab(low, own, high)
    for table, step_size in ((fine, FINE), (middle, MIDDLE), (coarse, COARSE)):
        for z in range(-DEPTH, 2 * DEPTH):
            alpha = get(3, z) * step_size
            table[0, z + DEPTH] = alpha
            table[1, z + DEPTH] = 1.0 - 6.0 * alpha
            for c in range(3):
                table[2 + c, z + DEPTH] = get(c, z) * step_size


def defects_kernel(low, own, high, fine, middle, out, one, two):
    def body(i, carry):
        start = slab(low, own, high, 3 * i)
        advance(start, writer(one), -3, 7, fine, FINE)
        advance(reader(one), writer(two), -2, 6, fine, FINE)
        advance(reader(two), writer(one), -1, 5, fine, FINE)

        def store(c, z, value):
            out[i, c, z] = value

        def subtract(c, z, value):
            out[i, c, z] = out[i, c, z] - value

        advance(reader(one), store, 0, 4, fine, FINE)
        advance(start, writer(two), -1, 5, middle, MIDDLE)
        advance(reader(two), subtract, 0, 4, middle, MIDDLE)
        return carry

    lax.fori_loop(0, 3, body, 0)


def opening_kernel(low, own, high, fine, defects, to_up, to_down, one, two):
    advance(slab(low, own, high), writer(one), -3, 7, fine, FINE)
    advance(reader(one), writer(two), -2, 6, fine, FINE)
    advance(reader(two), writer(one), -1, 5, fine, FINE)

    def store(c, z, value):
        to_up[c, z] = value
        to_down[c, z] = value

    advance(reader(one), store, 0, 4, fine, FINE)
    for c in range(3):
        for z in range(2):
            to_up[c, 4 + z] = defects[0, c, 2 + z]
            to_down[c, 4 + z] = defects[0, c, z]


def remainder_kernel(
    low, own, high, middle, coarse, defects, first, initial, defect, rest, late_up, late_down, kept, one
):
    start = slab(low, own, high)
    advance(start, writer(one), -1, 5, middle, MIDDLE)

    def subtract(c, z, value):
        defect[c, z] = first[c, z] - value

    advance(reader(one), subtract, 0, 4, middle, MIDDLE)
    advance(start, writer(one), -1, 5, coarse, COARSE)

    def subtract_rest(c, z, value):
        rest[c, z] = defects[2, c, z] - value

    advance(reader(one), subtract_rest, 0, 4, coarse, COARSE)
    for c in range(3):
        for z in range(DEPTH):
            late_up[c, z] = initial[c, z]
            late_down[c, z] = initial[c, z]
            kept[c, z] = initial[c, z]
        for z in range(2):
            late_up[c, 4 + z] = defect[c, 2 + z]
            late_down[c, 4 + z] = defect[c, z]


def second_kernel(low, own, high, middle, defects, rest, to_up, to_down, one, two):
    def added(c, z, value):
        if z < 0:
            term = low[c, 4 + 2 + z]
        elif z >= DEPTH:
            term = high[c, 4 + z - DEPTH]
        else:
            term = defects[0, c, z]
        two[c, z + DEPTH] = value + term

    def third(c, z, value):
        value = value + defects[1, c, z]
        to_up[c, z] = value
        to_down[c, z] = value

    advance(slab(low, own, high), writer(one), -3, 7, middle, MIDDLE)
    advance(reader(one), added, -2, 6, middle, MIDDLE)
    advance(reader(two), writer(one), -1, 5, middle, MIDDLE)
    advance(reader(one), third, 0, 4, middle, MIDDLE)
    for c in range(3):
        for z in range(2):
            to_up[c, 4 + z] = rest[c, 2 + z]
            to_down[c, 4 + z] = rest[c, z]


def coarse_defect_kernel(low, own, high, middle, rest, out, middle_out, one):
    def added(c, z, value):
        if z < 0:
            term = low[c, 4 + 2 + z]
        elif z >= DEPTH:
            term = high[c, 4 + z - DEPTH]
        else:
            term = rest[c, z]
        out[c, z + 2] = value + term
        if 0 <= z < DEPTH:
            middle_out[c, z] = value + term

    advance(slab(low, own, high), writer(one), -3, 7, middle, MIDDLE)
    advance(reader(one), added, -2, 6, middle, MIDDLE)


def take(kept, arrived):
    shift = (arrived.shape[1] - DEPTH) // 2
    for c in range(3):
        for z in range(DEPTH):
            kept[c, z] = arrived[c, z + shift]


def march_kernel(
    done, low, own, high, coarse, term_one, term_two, term, kept_in,
    state, message_one, message_two, kept, one, two,
):
    def first(c, z, value):
        value = value + term_one[c, z + 2]
        two[c, z + DEPTH] = value
        if 0 <= z + edge < message_one.shape[1]:
            message_one[c, z + edge] = value

    def second(c, z, value):
        value = value + term_two[c, z]
        state[c, z] = value
        message_two[c, z] = value

    edge = (message_one.shape[1] - DEPTH) // 2
    column = lax.axis_index("tm")
    marching = column == lax.axis_size("tm") - 1

    @pl.when(marching)
    def _():
        advance(slab(low, own, high), writer(one), -3, 7, coarse, COARSE)
        advance(reader(one), first, -2, 6, coarse, COARSE)
        advance(reader(two), writer(one), -1, 5, coarse, COARSE)
        advance(reader(one), second, 0, 4, coarse, COARSE)

    @pl.when(jnp.logical_not(marching))
    def _():
        for c in range(3):
            for z in range(message_one.shape[1]):
                message_one[c, z] = term[c, z + 2 - edge]
            for z in range(DEPTH):
                message_two[c, z] = term[c, z + 2]
                state[c, z] = own[c, z]

    if done[0] is not None:
        pl.when(column == done[0])(functools.partial(take, kept, term_one))
    if done[1] is not None:
        pl.when(column == done[1])(functools.partial(take, kept, term_two))


def last_march_kernel(done, low, own, high, coarse, term_one, kept, *rest):
    arrivals, (start, one) = rest[:-2], rest[-2:]
    column = lax.axis_index("tm")
    marching = column == lax.axis_size("tm") - 1

    def first(c, z, value):
        start[c, z] = value + term_one[c, z + 2]

    @pl.when(marching)
    def _():
        advance(slab(low, own, high), writer(one), -1, 5, coarse, COARSE)
        advance(reader(one), first, 0, 4, coarse, COARSE)

    pl.when(jnp.logical_not(marching))(functools.partial(take, start, kept))
    for t, arrived in zip(done, (term_one,) + arrivals):
        if t is not None:
            pl.when(column == t)(functools.partial(take, start, arrived))


def stations_kernel(low, own, high, middle, defect_low, defect, defect_high, defects, out, one, two):
    def first(c, z, value):
        if z < 0:
            term = defect_low[c, 4 + 2 + z]
        elif z >= DEPTH:
            term = defect_high[c, 4 + z - DEPTH]
        else:
            term = defect[c, z]
        value = value + term
        two[c, z + DEPTH] = value
        if 0 <= z < DEPTH:
            out[c, z] = value

    def second(c, z, value):
        out[3 + c, z] = value + defects[0, c, z]

    advance(slab(low, own, high), writer(one), -3, 7, middle, MIDDLE)
    advance(reader(one), first, -2, 6, middle, MIDDLE)
    advance(reader(two), writer(one), -1, 5, middle, MIDDLE)
    advance(reader(one), second, 0, 4, middle, MIDDLE)


def third_kernel(low, own, high, middle, defects, out, one):
    def third(c, z, value):
        out[c, z] = value + defects[1, c, z]

    advance(slab(low, own, high, 3), writer(one), -1, 5, middle, MIDDLE)
    advance(reader(one), third, 0, 4, middle, MIDDLE)


def fine_rows(start, fine, rows, at, one, two):
    def first(c, z, value):
        one[c, z + DEPTH] = value
        if 0 <= z < DEPTH:
            rows[at, c, z] = value

    def second(c, z, value):
        two[c, z + DEPTH] = value
        if 0 <= z < DEPTH:
            rows[at + 1, c, z] = value

    def third(c, z, value):
        rows[at + 2, c, z] = value

    advance(start, first, -2, 6, fine, FINE)
    advance(reader(one), second, -1, 5, fine, FINE)
    advance(reader(two), third, 0, 4, fine, FINE)


def send_rows(rows, result, sem, places):
    copies = [
        pltpu.make_async_copy(rows.at[at], result.at[place], sem.at[at])
        for at, place in enumerate(places)
    ]
    for copy in copies:
        copy.start()
    for copy in copies:
        copy.wait()


def first_rows_kernel(low, own, high, fine, coarse, term, stations, result, rows, one, two, sem):
    start = slab(low, own, high)
    fine_rows(start, fine, rows, 0, one, two)
    for c in range(3):
        for z in range(DEPTH):
            rows[3, c, z] = stations[c, z]
            rows[4, c, z] = stations[3 + c, z]

    def end(c, z, value):
        rows[5, c, z] = value + term[c, z + 2]

    advance(start, writer(one), -1, 5, coarse, COARSE)
    advance(reader(one), end, 0, 4, coarse, COARSE)
    send_rows(rows, result, sem, (0, 1, 2, 3, 7, 15))


def middle_rows_kernel(low, own, high, fine, station, before, result, rows, one, two, sem):
    for i in range(2):
        fine_rows(slab(low, own, high, 3 * i), fine, rows, 3 * i, one, two)
    for c in range(3):
        for z in range(DEPTH):
            rows[6, c, z] = station[c, z]
    send_rows(rows, result, sem, (4, 5, 6, 8, 9, 10, 11))


def last_rows_kernel(low, own, high, fine, before, result, rows, one, two, sem):
    fine_rows(slab(low, own, high), fine, rows, 0, one, two)
    send_rows(rows, result, sem, (12, 13, 14))


def permute(x, moves):
    spaces = lax.axis_size("space")
    times = lax.axis_size("tm")
    pairs = []
    for t in range(times):
        if t in moves:
            target, by = moves[t]
            pairs += [(t * spaces + s, target * spaces + (s + by) % spaces) for s in range(spaces)]
        else:
            pairs += [(t * spaces + s, t * spaces + (s ^ 1)) for s in range(spaces)]
    return lax.ppermute(x, AXES, pairs)


def halos(to_up, to_down, columns):
    return (
        permute(to_up, {t: (t, 1) for t in columns}),
        permute(to_down, {t: (t, -1) for t in columns}),
    )


def cycle(x, *columns):
    return permute(x, {t: (after, 0) for t, after in zip(columns, columns[1:] + columns[:1])})


PLANE = (16, 128)
WORK = pltpu.VMEM((3, 3 * DEPTH) + PLANE, jnp.float32)
VMEM_SPEC = pl.BlockSpec(memory_space=pltpu.VMEM)


def call(kernel, shapes, inputs, works, units, aliases=None):
    outs = [jax.ShapeDtypeStruct(tuple(shape) + PLANE, jnp.float32) for shape in shapes]
    result = pl.pallas_call(
        kernel,
        out_shape=outs,
        in_specs=[VMEM_SPEC] * len(inputs),
        out_specs=[VMEM_SPEC] * len(outs),
        scratch_shapes=[WORK] * works,
        input_output_aliases=aliases or {},
        compiler_params=pltpu.CompilerParams(vmem_limit_bytes=8 << 20),
        cost_estimate=pl.CostEstimate(flops=units * 120000, bytes_accessed=units * 60000, transcendentals=0),
    )(*inputs)
    return result[0] if len(outs) == 1 else result


def emit(kernel, inputs, count, before, units):
    specs = [VMEM_SPEC] * len(inputs)
    if before is not None:
        inputs = list(inputs) + [before]
        specs.append(pl.BlockSpec(memory_space=pl.ANY))
    return pl.pallas_call(
        kernel,
        out_shape=jax.ShapeDtypeStruct((16, 3, DEPTH) + PLANE, jnp.float32),
        in_specs=specs,
        out_specs=pl.BlockSpec(memory_space=pl.ANY),
        scratch_shapes=[pltpu.VMEM((count, 3, DEPTH) + PLANE, jnp.float32), WORK, WORK, pltpu.SemaphoreType.DMA((count,))],
        input_output_aliases={} if before is None else {len(inputs) - 1: 0},
        compiler_params=pltpu.CompilerParams(vmem_limit_bytes=8 << 20),
        cost_estimate=pl.CostEstimate(flops=units * 120000, bytes_accessed=units * 60000, transcendentals=0),
    )(*inputs)


def on_device(initial, guesses, viscosity, forcing):
    times = lax.axis_size("tm")
    column = lax.axis_index("tm")
    every = range(times)
    marcher = times - 1
    alone = (marcher,)

    last, guesses = lax.optimization_barrier((guesses[3], guesses))
    members = guesses[:3].reshape((9,) + guesses.shape[2:])
    incoming = permute(last, {t: ((t + 1) % times, 0) for t in every})
    member_low, member_high = halos(members, members, every)
    fields = jnp.concatenate([forcing, viscosity[None]], axis=0)
    field_low, field_high = halos(fields, fields, every)
    opening = jnp.where(column == 0, initial, incoming)
    open_low, open_high = halos(opening, opening, every)

    table = (5, 3 * DEPTH)
    fine, middle, coarse = call(tables_kernel, [table] * 3, [field_low, fields, field_high], 0, 10)
    defects = call(defects_kernel, [(3, 3, DEPTH)], [member_low, members, member_high, fine, middle], 2, 114)
    to_up, to_down = call(opening_kernel, [(3, 6)] * 2, [open_low, opening, open_high, fine, defects], 2, 28)
    low, high = halos(to_up, to_down, every)
    defect, rest, late_up, late_down, kept = call(
        remainder_kernel,
        [(3, DEPTH)] * 2 + [(3, 6)] * 2 + [(3, DEPTH)],
        [open_low, opening, open_high, middle, coarse, defects, to_up, initial],
        1,
        20,
    )
    second_up, second_down = call(second_kernel, [(3, 6)] * 2, [low, to_up, high, middle, defects, rest], 2, 28)
    rest_low, rest_high = halos(second_up, second_down, every)
    term, term_middle = call(
        coarse_defect_kernel, [(3, 8), (3, DEPTH)], [rest_low, second_up, rest_high, middle, rest], 1, 18
    )

    terms = {marcher: term}
    ahead = (term, term_middle)
    for t in range(min(6, marcher)):
        if t == 4:
            ahead = lax.optimization_barrier((term, term_middle, terms[0], terms[1]))
            ahead, (terms[0], terms[1]) = ahead[:2], ahead[2:]
        terms[t] = cycle(ahead[t % 2], t, marcher)
    late_low, late_high = halos(late_up, late_down, every)
    state, low, high = late_up, late_low, late_high
    brought, extra = {}, {}
    messages = None
    for period in range(times // 2):
        if period:
            low, high = halos(state, state, alone)
            for i in range(2):
                t = 2 * period + 6 + i
                done = 2 * period - 1 + i
                if period == 1 and t - 2 < marcher:
                    terms[t - 2] = cycle(messages[i], t - 2, marcher)
                if t < marcher:
                    terms[t] = cycle(messages[i], t, marcher, done)
                    brought[t] = done
                else:
                    extra[done] = cycle(messages[i], marcher, done)
        if 2 * period + 2 < times:
            pair = (2 * period, 2 * period + 1)
            state, *messages, kept = call(
                functools.partial(march_kernel, [brought.get(t) for t in pair]),
                [(3, DEPTH), (3, 8 if 2 * period + 8 < marcher else DEPTH), (3, DEPTH), (3, DEPTH)],
                [low, state, high, coarse, terms[pair[0]], terms[pair[1]], term, kept],
                2,
                28,
                {7: 3},
            )
        else:
            start = call(
                functools.partial(last_march_kernel, [brought.get(2 * period)] + list(extra)),
                [(3, DEPTH)],
                [low, state, high, coarse, terms[2 * period], kept] + list(extra.values()),
                1,
                10,
            )

    low, high = halos(start, start, every)
    stations = call(
        stations_kernel, [(6, DEPTH)], [low, start, high, middle, late_low, defect, late_high, defects], 2, 28
    )
    station_low, station_high = halos(stations, stations, every)
    result = emit(first_rows_kernel, [low, start, high, fine, coarse, term, stations], 6, None, 28)
    third = call(third_kernel, [(3, DEPTH)], [station_low, stations, station_high, middle, defects], 1, 10)
    third_low, third_high = halos(third, third, every)
    result = emit(middle_rows_kernel, [station_low, stations, station_high, fine, third], 7, result, 36)
    return emit(last_rows_kernel, [third_low, third, third_high, fine], 3, result, 18)


def solution(mesh):
    return jax.shard_map(
        on_device,
        mesh=mesh,
        in_specs=(
            P(None, "space", None, None),
            P("tm", None, "space", None, None),
            P("space", None, None),
            P(None, "space", None, None),
        ),
        out_specs=P("tm", None, "space", None, None),
        check_vma=False,
    )
```

```python
import functools

import jax
import jax.numpy as jnp
from jax import lax
from jax.experimental import pallas as pl
from jax.experimental.pallas import tpu as pltpu
from jax.sharding import PartitionSpec as P


time_step = 0.019
FINE, MIDDLE, COARSE = time_step, 2.0 * time_step, 8.0 * time_step
DEPTH = 4
AXES = ("tm", "space")


def slab(low, own, high, base=0):
    def get(c, z):
        if z < 0:
            return low[base + c, z + DEPTH]
        if z >= DEPTH:
            return high[base + c, z - DEPTH]
        return own[base + c, z]

    return get


def reader(ref, shift=DEPTH):
    return lambda c, z: ref[c, z + shift]


def writer(ref, shift=DEPTH):
    def put(c, z, value):
        ref[c, z + shift] = value

    return put


def advance(get, put, first, last, table, step_size):
    for z in range(first, last):
        alpha = table[0, z + DEPTH]
        keep = table[1, z + DEPTH]
        center = [get(c, z) for c in range(3)]
        half = [value * (0.5 * step_size) for value in center]
        east, west = alpha - half[0], alpha + half[0]
        north, south = alpha - half[1], alpha + half[1]
        up, down = alpha - half[2], alpha + half[2]
        for c in range(3):
            value = center[c]
            along_x = east * pltpu.roll(value, 127, 1) + west * pltpu.roll(value, 1, 1)
            along_y = north * pltpu.roll(value, 15, 0) + south * pltpu.roll(value, 1, 0)
            along_z = up * get(c, z + 1) + down * get(c, z - 1)
            put(c, z, (keep * value + table[2 + c, z + DEPTH]) + along_x + (along_y + along_z))


def tables_kernel(low, own, high, fine, middle, coarse):
    get = slab(low, own, high)
    for table, step_size in ((fine, FINE), (middle, MIDDLE), (coarse, COARSE)):
        for z in range(-DEPTH, 2 * DEPTH):
            alpha = get(3, z) * step_size
            table[0, z + DEPTH] = alpha
            table[1, z + DEPTH] = 1.0 - 6.0 * alpha
            for c in range(3):
                table[2 + c, z + DEPTH] = get(c, z) * step_size


def defects_kernel(low, own, high, fine, middle, out, one, two):
    def body(i, carry):
        start = slab(low, own, high, 3 * i)
        advance(start, writer(one), -3, 7, fine, FINE)
        advance(reader(one), writer(two), -2, 6, fine, FINE)
        advance(reader(two), writer(one), -1, 5, fine, FINE)

        def store(c, z, value):
            out[i, c, z] = value

        def subtract(c, z, value):
            out[i, c, z] = out[i, c, z] - value

        advance(reader(one), store, 0, 4, fine, FINE)
        advance(start, writer(two), -1, 5, middle, MIDDLE)
        advance(reader(two), subtract, 0, 4, middle, MIDDLE)
        return carry

    lax.fori_loop(0, 3, body, 0)


def opening_kernel(low, own, high, fine, defects, to_up, to_down, one, two):
    advance(slab(low, own, high), writer(one), -3, 7, fine, FINE)
    advance(reader(one), writer(two), -2, 6, fine, FINE)
    advance(reader(two), writer(one), -1, 5, fine, FINE)

    def store(c, z, value):
        to_up[c, z] = value
        to_down[c, z] = value

    advance(reader(one), store, 0, 4, fine, FINE)
    for c in range(3):
        for z in range(2):
            to_up[c, 4 + z] = defects[0, c, 2 + z]
            to_down[c, 4 + z] = defects[0, c, z]


def remainder_kernel(
    low, own, high, middle, coarse, defects, first, initial, defect, rest, late_up, late_down, kept, one
):
    start = slab(low, own, high)
    advance(start, writer(one), -1, 5, middle, MIDDLE)

    def subtract(c, z, value):
        defect[c, z] = first[c, z] - value

    advance(reader(one), subtract, 0, 4, middle, MIDDLE)
    advance(start, writer(one), -1, 5, coarse, COARSE)

    def subtract_rest(c, z, value):
        rest[c, z] = defects[2, c, z] - value

    advance(reader(one), subtract_rest, 0, 4, coarse, COARSE)
    for c in range(3):
        for z in range(DEPTH):
            late_up[c, z] = initial[c, z]
            late_down[c, z] = initial[c, z]
            kept[c, z] = initial[c, z]
        for z in range(2):
            late_up[c, 4 + z] = defect[c, 2 + z]
            late_down[c, 4 + z] = defect[c, z]


def second_kernel(low, own, high, middle, defects, rest, to_up, to_down, one, two):
    def added(c, z, value):
        if z < 0:
            term = low[c, 4 + 2 + z]
        elif z >= DEPTH:
            term = high[c, 4 + z - DEPTH]
        else:
            term = defects[0, c, z]
        two[c, z + DEPTH] = value + term

    def third(c, z, value):
        value = value + defects[1, c, z]
        to_up[c, z] = value
        to_down[c, z] = value

    advance(slab(low, own, high), writer(one), -3, 7, middle, MIDDLE)
    advance(reader(one), added, -2, 6, middle, MIDDLE)
    advance(reader(two), writer(one), -1, 5, middle, MIDDLE)
    advance(reader(one), third, 0, 4, middle, MIDDLE)
    for c in range(3):
        for z in range(2):
            to_up[c, 4 + z] = rest[c, 2 + z]
            to_down[c, 4 + z] = rest[c, z]


def coarse_defect_kernel(low, own, high, middle, rest, out, middle_out, one):
    def added(c, z, value):
        if z < 0:
            term = low[c, 4 + 2 + z]
        elif z >= DEPTH:
            term = high[c, 4 + z - DEPTH]
        else:
            term = rest[c, z]
        out[c, z + 2] = value + term
        if 0 <= z < DEPTH:
            middle_out[c, z] = value + term

    advance(slab(low, own, high), writer(one), -3, 7, middle, MIDDLE)
    advance(reader(one), added, -2, 6, middle, MIDDLE)


def take(kept, arrived):
    shift = (arrived.shape[1] - DEPTH) // 2
    for c in range(3):
        for z in range(DEPTH):
            kept[c, z] = arrived[c, z + shift]


def march_kernel(
    done, low, own, high, coarse, term_one, term_two, term, kept_in,
    state, message_one, message_two, kept, one, two,
):
    def first(c, z, value):
        value = value + term_one[c, z + 2]
        two[c, z + DEPTH] = value
        if 0 <= z + edge < message_one.shape[1]:
            message_one[c, z + edge] = value

    def second(c, z, value):
        value = value + term_two[c, z]
        state[c, z] = value
        message_two[c, z] = value

    edge = (message_one.shape[1] - DEPTH) // 2
    column = lax.axis_index("tm")
    marching = column == lax.axis_size("tm") - 1

    @pl.when(marching)
    def _():
        advance(slab(low, own, high), writer(one), -3, 7, coarse, COARSE)
        advance(reader(one), first, -2, 6, coarse, COARSE)
        advance(reader(two), writer(one), -1, 5, coarse, COARSE)
        advance(reader(one), second, 0, 4, coarse, COARSE)

    @pl.when(jnp.logical_not(marching))
    def _():
        for c in range(3):
            for z in range(message_one.shape[1]):
                message_one[c, z] = term[c, z + 2 - edge]
            for z in range(DEPTH):
                message_two[c, z] = term[c, z + 2]
                state[c, z] = own[c, z]

    if done[0] is not None:
        pl.when(column == done[0])(functools.partial(take, kept, term_one))
    if done[1] is not None:
        pl.when(column == done[1])(functools.partial(take, kept, term_two))


def last_march_kernel(done, low, own, high, coarse, term_one, kept, *rest):
    arrivals, (start, one) = rest[:-2], rest[-2:]
    column = lax.axis_index("tm")
    marching = column == lax.axis_size("tm") - 1

    def first(c, z, value):
        start[c, z] = value + term_one[c, z + 2]

    @pl.when(marching)
    def _():
        advance(slab(low, own, high), writer(one), -1, 5, coarse, COARSE)
        advance(reader(one), first, 0, 4, coarse, COARSE)

    pl.when(jnp.logical_not(marching))(functools.partial(take, start, kept))
    for t, arrived in zip(done, (term_one,) + arrivals):
        if t is not None:
            pl.when(column == t)(functools.partial(take, start, arrived))


def stations_kernel(low, own, high, middle, defect_low, defect, defect_high, defects, out, one, two):
    def first(c, z, value):
        if z < 0:
            term = defect_low[c, 4 + 2 + z]
        elif z >= DEPTH:
            term = defect_high[c, 4 + z - DEPTH]
        else:
            term = defect[c, z]
        value = value + term
        two[c, z + DEPTH] = value
        if 0 <= z < DEPTH:
            out[c, z] = value

    def second(c, z, value):
        out[3 + c, z] = value + defects[0, c, z]

    advance(slab(low, own, high), writer(one), -3, 7, middle, MIDDLE)
    advance(reader(one), first, -2, 6, middle, MIDDLE)
    advance(reader(two), writer(one), -1, 5, middle, MIDDLE)
    advance(reader(one), second, 0, 4, middle, MIDDLE)


def third_kernel(low, own, high, middle, defects, out, one):
    def third(c, z, value):
        out[c, z] = value + defects[1, c, z]

    advance(slab(low, own, high, 3), writer(one), -1, 5, middle, MIDDLE)
    advance(reader(one), third, 0, 4, middle, MIDDLE)


def fine_rows(start, fine, rows, at, one, two):
    def first(c, z, value):
        one[c, z + DEPTH] = value
        if 0 <= z < DEPTH:
            rows[at, c, z] = value

    def second(c, z, value):
        two[c, z + DEPTH] = value
        if 0 <= z < DEPTH:
            rows[at + 1, c, z] = value

    def third(c, z, value):
        rows[at + 2, c, z] = value

    advance(start, first, -2, 6, fine, FINE)
    advance(reader(one), second, -1, 5, fine, FINE)
    advance(reader(two), third, 0, 4, fine, FINE)


def send_rows(rows, result, sem, places):
    copies = [
        pltpu.make_async_copy(rows.at[at], result.at[place], sem.at[at])
        for at, place in enumerate(places)
    ]
    for copy in copies:
        copy.start()
    for copy in copies:
        copy.wait()


def first_rows_kernel(low, own, high, fine, coarse, term, stations, result, rows, one, two, sem):
    start = slab(low, own, high)
    fine_rows(start, fine, rows, 0, one, two)
    for c in range(3):
        for z in range(DEPTH):
            rows[3, c, z] = stations[c, z]
            rows[4, c, z] = stations[3 + c, z]

    def end(c, z, value):
        rows[5, c, z] = value + term[c, z + 2]

    advance(start, writer(one), -1, 5, coarse, COARSE)
    advance(reader(one), end, 0, 4, coarse, COARSE)
    send_rows(rows, result, sem, (0, 1, 2, 3, 7, 15))


def middle_rows_kernel(low, own, high, fine, station, before, result, rows, one, two, sem):
    for i in range(2):
        fine_rows(slab(low, own, high, 3 * i), fine, rows, 3 * i, one, two)
    for c in range(3):
        for z in range(DEPTH):
            rows[6, c, z] = station[c, z]
    send_rows(rows, result, sem, (4, 5, 6, 8, 9, 10, 11))


def last_rows_kernel(low, own, high, fine, before, result, rows, one, two, sem):
    fine_rows(slab(low, own, high), fine, rows, 0, one, two)
    send_rows(rows, result, sem, (12, 13, 14))


def permute(x, moves):
    spaces = lax.axis_size("space")
    times = lax.axis_size("tm")
    pairs = []
    for t in range(times):
        if t in moves:
            target, by = moves[t]
            pairs += [(t * spaces + s, target * spaces + (s + by) % spaces) for s in range(spaces)]
        else:
            pairs += [(t * spaces + s, t * spaces + (s ^ 1)) for s in range(spaces)]
    return lax.ppermute(x, AXES, pairs)


def halos(to_up, to_down, columns):
    return (
        permute(to_up, {t: (t, 1) for t in columns}),
        permute(to_down, {t: (t, -1) for t in columns}),
    )


def cycle(x, *columns):
    return permute(x, {t: (after, 0) for t, after in zip(columns, columns[1:] + columns[:1])})


PLANE = (16, 128)
WORK = pltpu.VMEM((3, 3 * DEPTH) + PLANE, jnp.float32)
VMEM_SPEC = pl.BlockSpec(memory_space=pltpu.VMEM)


def call(kernel, shapes, inputs, works, units, aliases=None):
    outs = [jax.ShapeDtypeStruct(tuple(shape) + PLANE, jnp.float32) for shape in shapes]
    result = pl.pallas_call(
        kernel,
        out_shape=outs,
        in_specs=[VMEM_SPEC] * len(inputs),
        out_specs=[VMEM_SPEC] * len(outs),
        scratch_shapes=[WORK] * works,
        input_output_aliases=aliases or {},
        compiler_params=pltpu.CompilerParams(vmem_limit_bytes=8 << 20),
        cost_estimate=pl.CostEstimate(flops=units * 120000, bytes_accessed=units * 60000, transcendentals=0),
    )(*inputs)
    return result[0] if len(outs) == 1 else result


def emit(kernel, inputs, count, before, units):
    specs = [VMEM_SPEC] * len(inputs)
    if before is not None:
        inputs = list(inputs) + [before]
        specs.append(pl.BlockSpec(memory_space=pl.ANY))
    return pl.pallas_call(
        kernel,
        out_shape=jax.ShapeDtypeStruct((16, 3, DEPTH) + PLANE, jnp.float32),
        in_specs=specs,
        out_specs=pl.BlockSpec(memory_space=pl.ANY),
        scratch_shapes=[pltpu.VMEM((count, 3, DEPTH) + PLANE, jnp.float32), WORK, WORK, pltpu.SemaphoreType.DMA((count,))],
        input_output_aliases={} if before is None else {len(inputs) - 1: 0},
        compiler_params=pltpu.CompilerParams(vmem_limit_bytes=8 << 20),
        cost_estimate=pl.CostEstimate(flops=units * 120000, bytes_accessed=units * 60000, transcendentals=0),
    )(*inputs)


def cycle_pass(initial, guesses, viscosity, forcing):
    times = lax.axis_size("tm")
    column = lax.axis_index("tm")
    every = range(times)
    marcher = times - 1
    alone = (marcher,)

    last, guesses = lax.optimization_barrier((guesses[3], guesses))
    members = guesses[:3].reshape((9,) + guesses.shape[2:])
    incoming = permute(last, {t: ((t + 1) % times, 0) for t in every})
    member_low, member_high = halos(members, members, every)
    fields = jnp.concatenate([forcing, viscosity[None]], axis=0)
    field_low, field_high = halos(fields, fields, every)
    opening = jnp.where(column == 0, initial, incoming)
    open_low, open_high = halos(opening, opening, every)

    table = (5, 3 * DEPTH)
    fine, middle, coarse = call(tables_kernel, [table] * 3, [field_low, fields, field_high], 0, 10)
    defects = call(defects_kernel, [(3, 3, DEPTH)], [member_low, members, member_high, fine, middle], 2, 114)
    to_up, to_down = call(opening_kernel, [(3, 6)] * 2, [open_low, opening, open_high, fine, defects], 2, 28)
    low, high = halos(to_up, to_down, every)
    defect, rest, late_up, late_down, kept = call(
        remainder_kernel,
        [(3, DEPTH)] * 2 + [(3, 6)] * 2 + [(3, DEPTH)],
        [open_low, opening, open_high, middle, coarse, defects, to_up, initial],
        1,
        20,
    )
    second_up, second_down = call(second_kernel, [(3, 6)] * 2, [low, to_up, high, middle, defects, rest], 2, 28)
    rest_low, rest_high = halos(second_up, second_down, every)
    term, term_middle = call(
        coarse_defect_kernel, [(3, 8), (3, DEPTH)], [rest_low, second_up, rest_high, middle, rest], 1, 18
    )

    terms = {marcher: term}
    ahead = (term, term_middle)
    for t in range(min(6, marcher)):
        if t == 4:
            ahead = lax.optimization_barrier((term, term_middle, terms[0], terms[1]))
            ahead, (terms[0], terms[1]) = ahead[:2], ahead[2:]
        terms[t] = cycle(ahead[t % 2], t, marcher)
    late_low, late_high = halos(late_up, late_down, every)
    state, low, high = late_up, late_low, late_high
    brought, extra = {}, {}
    messages = None
    for period in range(times // 2):
        if period:
            low, high = halos(state, state, alone)
            for i in range(2):
                t = 2 * period + 6 + i
                done = 2 * period - 1 + i
                if period == 1 and t - 2 < marcher:
                    terms[t - 2] = cycle(messages[i], t - 2, marcher)
                if t < marcher:
                    terms[t] = cycle(messages[i], t, marcher, done)
                    brought[t] = done
                else:
                    extra[done] = cycle(messages[i], marcher, done)
        if 2 * period + 2 < times:
            pair = (2 * period, 2 * period + 1)
            wide = 8 if 2 * period + 8 < marcher else DEPTH
            state, *messages, kept = call(
                functools.partial(march_kernel, [brought.get(t) for t in pair]),
                [(3, DEPTH), (3, wide), (3, DEPTH), (3, DEPTH)],
                [low, state, high, coarse, terms[pair[0]], terms[pair[1]], term, kept],
                2,
                28,
                {7: 3},
            )
        else:
            start = call(
                functools.partial(last_march_kernel, [brought.get(2 * period)] + list(extra)),
                [(3, DEPTH)],
                [low, state, high, coarse, terms[2 * period], kept] + list(extra.values()),
                1,
                10,
            )

    low, high = halos(start, start, every)
    stations = call(
        stations_kernel, [(6, DEPTH)], [low, start, high, middle, late_low, defect, late_high, defects], 2, 28
    )
    station_low, station_high = halos(stations, stations, every)
    result = emit(first_rows_kernel, [low, start, high, fine, coarse, term, stations], 6, None, 28)
    third = call(third_kernel, [(3, DEPTH)], [station_low, stations, station_high, middle, defects], 1, 10)
    third_low, third_high = halos(third, third, every)
    result = emit(middle_rows_kernel, [station_low, stations, station_high, fine, third], 7, result, 36)
    return emit(last_rows_kernel, [third_low, third, third_high, fine], 3, result, 18)


def solution(mesh):
    return jax.shard_map(
        cycle_pass,
        mesh=mesh,
        in_specs=(
            P(None, "space", None, None),
            P("tm", None, "space", None, None),
            P("space", None, None),
            P(None, "space", None, None),
        ),
        out_specs=P("tm", None, "space", None, None),
        check_vma=False,
    )
```

```python
import functools

import jax
import jax.numpy as jnp
from jax import lax
from jax.experimental import pallas as pl
from jax.experimental.pallas import tpu as pltpu
from jax.sharding import PartitionSpec as P


time_step = 0.019
FINE, MIDDLE, COARSE = time_step, 2.0 * time_step, 8.0 * time_step
DEPTH = 4
AXES = ("tm", "space")


def slab(low, own, high, base=0):
    def get(c, z):
        if z < 0:
            return low[base + c, z + DEPTH]
        if z >= DEPTH:
            return high[base + c, z - DEPTH]
        return own[base + c, z]

    return get


def deep_slab(lower, low, own, high, higher, lowest=None, highest=None):
    near = slab(low, own, high)

    def get(c, z):
        if z < -2 * DEPTH:
            return lowest[c, 0]
        if z < -DEPTH:
            return lower[c, z + 2 * DEPTH]
        if z >= 3 * DEPTH:
            return highest[c, 0]
        if z >= 2 * DEPTH:
            return higher[c, z - 2 * DEPTH]
        return near(c, z)

    return get


def reader(ref, shift=DEPTH):
    return lambda c, z: ref[c, z + shift]


def writer(ref, shift=DEPTH):
    def put(c, z, value):
        ref[c, z + shift] = value

    return put


def advance(get, put, first, last, table, step_size):
    edge = (table.shape[1] - DEPTH) // 2
    for z in range(first, last) if isinstance(first, int) else [first + i for i in range(last)]:
        alpha = table[0, z + edge]
        keep = table[1, z + edge]
        center = [get(c, z) for c in range(3)]
        half = [value * (0.5 * step_size) for value in center]
        east, west = alpha - half[0], alpha + half[0]
        north, south = alpha - half[1], alpha + half[1]
        up, down = alpha - half[2], alpha + half[2]
        for c in range(3):
            value = center[c]
            along_x = east * pltpu.roll(value, 127, 1) + west * pltpu.roll(value, 1, 1)
            along_y = north * pltpu.roll(value, 15, 0) + south * pltpu.roll(value, 1, 0)
            along_z = up * get(c, z + 1) + down * get(c, z - 1)
            put(c, z, (keep * value + table[2 + c, z + edge]) + along_x + (along_y + along_z))


def advance_halves(get, put, first, last, table, step_size):
    count = (last - first) // 2

    def body(i, carry):
        advance(get, put, first + i * count, count, table, step_size)
        return carry

    lax.fori_loop(0, 2, body, 0)


def fill(get, table, step_size):
    edge = (table.shape[1] - DEPTH) // 2
    for z in range(-edge, DEPTH + edge):
        alpha = get(3, z) * step_size
        table[0, z + edge] = alpha
        table[1, z + edge] = 1.0 - 6.0 * alpha
        for c in range(3):
            table[2 + c, z + edge] = get(c, z) * step_size


def tables_kernel(low, own, high, fine, middle, coarse):
    get = slab(low, own, high)
    for table, step_size in ((fine, FINE), (middle, MIDDLE), (coarse, COARSE)):
        fill(get, table, step_size)


def wide_table_kernel(lower, low, own, high, higher, middle):
    fill(deep_slab(lower, low, own, high, higher), middle, MIDDLE)


def defects_kernel(low, own, high, fine, middle, out, one, two):
    def body(i, carry):
        start = slab(low, own, high, 3 * (i + 1))
        advance(start, writer(one), -3, 7, fine, FINE)
        advance(reader(one), writer(two), -2, 6, fine, FINE)
        advance(reader(two), writer(one), -1, 5, fine, FINE)

        def store(c, z, value):
            out[i, c, z] = value

        def subtract(c, z, value):
            out[i, c, z] = out[i, c, z] - value

        advance(reader(one), store, 0, 4, fine, FINE)
        advance(start, writer(two), -1, 5, middle, MIDDLE)
        advance(reader(two), subtract, 0, 4, middle, MIDDLE)
        return carry

    lax.fori_loop(0, out.shape[0], body, 0)


def opening_kernel(
    member_low, members, member_high, low, own, high, fine, middle, next_one, to_up, to_down,
    one, two, both, moved,
):
    near = slab(member_low, members, member_high)
    for get, base in ((near, 0), (slab(low, own, high), 3)):
        for c in range(3):
            for z in range(-DEPTH, 2 * DEPTH):
                both[base + c, z + DEPTH] = get(c, z)

    def body(i, carry):
        def store(c, z, value):
            moved[3 * i + c, z] = value

        advance(lambda c, z: both[3 * i + c, z + DEPTH], writer(one), -3, 7, fine, FINE)
        advance(reader(one), writer(two), -2, 6, fine, FINE)
        advance(reader(two), writer(one), -1, 5, fine, FINE)
        advance(reader(one), store, 0, 4, fine, FINE)
        return carry

    lax.fori_loop(0, 2, body, 0)

    def subtract(c, z, value):
        next_one[0, c, z] = moved[c, z] - value

    advance(near, writer(one), -1, 5, middle, MIDDLE)
    advance(reader(one), subtract, 0, 4, middle, MIDDLE)
    for c in range(3):
        for z in range(DEPTH):
            to_up[c, z] = moved[3 + c, z]
            to_down[c, z] = moved[3 + c, z]
        for z in range(2):
            to_up[c, 4 + z] = next_one[0, c, 2 + z]
            to_down[c, 4 + z] = next_one[0, c, z]


def remainder_kernel(
    low, own, high, middle, coarse, next_one, others, first, initial, fields,
    defect, rest, late, deep_up, deep_down, kept, one,
):
    start = slab(low, own, high)
    advance(start, writer(one), -1, 5, middle, MIDDLE)

    def subtract(c, z, value):
        value = first[c, z] - value
        defect[c, z] = value
        late[3 + c, z] = value
        if z > 0:
            deep_up[4 + c, z - 1] = value
        if z < 3:
            deep_down[4 + c, z] = value

    advance(reader(one), subtract, 0, 4, middle, MIDDLE)
    advance(start, writer(one), -1, 5, coarse, COARSE)

    def subtract_rest(c, z, value):
        rest[c, z] = others[1, c, z] - value

    advance(reader(one), subtract_rest, 0, 4, coarse, COARSE)
    for c in range(3):
        for z in range(DEPTH):
            late[c, z] = initial[c, z]
            late[6 + c, z] = next_one[0, c, z]
            late[9 + c, z] = others[0, c, z]
            kept[c, z] = initial[c, z]
        deep_up[4 + c, 3] = next_one[0, c, 3]
        deep_down[4 + c, 3] = next_one[0, c, 0]
    for c in range(4):
        for z in range(DEPTH):
            deep_up[c, z] = fields[c, z]
            deep_down[c, z] = fields[c, z]


def second_kernel(low, own, high, middle, defects, others, rest, to_up, to_down, one, two):
    def added(c, z, value):
        if z < 0:
            term = low[c, 4 + 2 + z]
        elif z >= DEPTH:
            term = high[c, 4 + z - DEPTH]
        else:
            term = defects[0, c, z]
        two[c, z + DEPTH] = value + term

    def third(c, z, value):
        value = value + others[0, c, z]
        to_up[c, z] = value
        to_down[c, z] = value

    advance(slab(low, own, high), writer(one), -3, 7, middle, MIDDLE)
    advance(reader(one), added, -2, 6, middle, MIDDLE)
    advance(reader(two), writer(one), -1, 5, middle, MIDDLE)
    advance(reader(one), third, 0, 4, middle, MIDDLE)
    for c in range(3):
        for z in range(2):
            to_up[c, 4 + z] = rest[c, 2 + z]
            to_down[c, 4 + z] = rest[c, z]


def coarse_defect_kernel(low, own, high, middle, rest, out, middle_out, one):
    def added(c, z, value):
        if z < 0:
            term = low[c, 4 + 2 + z]
        elif z >= DEPTH:
            term = high[c, 4 + z - DEPTH]
        else:
            term = rest[c, z]
        out[c, z + 2] = value + term
        if 0 <= z < DEPTH:
            middle_out[c, z] = value + term

    advance(slab(low, own, high), writer(one), -3, 7, middle, MIDDLE)
    advance(reader(one), added, -2, 6, middle, MIDDLE)


def take(kept, arrived):
    shift = (arrived.shape[1] - DEPTH) // 2
    for c in range(3):
        for z in range(DEPTH):
            kept[c, z] = arrived[c, z + shift]


def march_kernel(
    done, low, own, high, coarse, term_one, term_two, term, kept_in,
    state, message_one, message_two, kept, one, two,
):
    def first(c, z, value):
        value = value + term_one[c, z + 2]
        two[c, z + DEPTH] = value
        if 0 <= z + edge < message_one.shape[1]:
            message_one[c, z + edge] = value

    def second(c, z, value):
        value = value + term_two[c, z]
        state[c, z] = value
        message_two[c, z] = value

    edge = (message_one.shape[1] - DEPTH) // 2
    column = lax.axis_index("tm")
    marching = column == lax.axis_size("tm") - 1

    @pl.when(marching)
    def _():
        advance(slab(low, own, high), writer(one), -3, 7, coarse, COARSE)
        advance(reader(one), first, -2, 6, coarse, COARSE)
        advance(reader(two), writer(one), -1, 5, coarse, COARSE)
        advance(reader(one), second, 0, 4, coarse, COARSE)

    @pl.when(jnp.logical_not(marching))
    def _():
        for c in range(3):
            for z in range(message_one.shape[1]):
                message_one[c, z] = term[c, z + 2 - edge]
            for z in range(DEPTH):
                message_two[c, z] = term[c, z + 2]
                state[c, z] = own[c, z]

    if done[0] is not None:
        pl.when(column == done[0])(functools.partial(take, kept, term_one))
    if done[1] is not None:
        pl.when(column == done[1])(functools.partial(take, kept, term_two))


def last_march_kernel(done, low, own, high, coarse, term_one, kept, *rest):
    arrivals, (start, one) = rest[:-2], rest[-2:]
    column = lax.axis_index("tm")
    marching = column == lax.axis_size("tm") - 1

    def first(c, z, value):
        start[c, z] = value + term_one[c, z + 2]

    @pl.when(marching)
    def _():
        advance(slab(low, own, high), writer(one), -1, 5, coarse, COARSE)
        advance(reader(one), first, 0, 4, coarse, COARSE)

    pl.when(jnp.logical_not(marching))(functools.partial(take, start, kept))
    for t, arrived in zip(done, (term_one,) + arrivals):
        if t is not None:
            pl.when(column == t)(functools.partial(take, start, arrived))


SHIFT = 2 * DEPTH + 2
FINE_SHIFT = 3


def finish_kernel(
    lowest, lower, low, own, high, higher, highest, fine, middle, coarse, term,
    deep_low, late_low, late, late_high, deep_high, result, rows, one, station, anchors, two, sem,
):
    def copy(i):
        return pltpu.make_async_copy(rows.at[i], result.at[i], sem.at[i])

    start = deep_slab(lower, low, own, high, higher, lowest, highest)
    near = slab(late_low, late, late_high, 3)
    for c in range(3):
        for z in range(-FINE_SHIFT, DEPTH + FINE_SHIFT):
            anchors[c, z + FINE_SHIFT] = start(c, z)

    def end(c, z, value):
        rows[15, c, z] = value + term[c, z + 2]

    advance(start, writer(one, SHIFT), -1, 5, coarse, COARSE)
    advance(reader(one, SHIFT), end, 0, 4, coarse, COARSE)
    copy(15).start()

    for number in range(3):
        reach = 7 - 2 * number

        def store(c, z, value):
            if z < -DEPTH:
                value = value + (deep_low[4 + c, 3] if number else deep_low[4 + c, z + 7])
            elif z >= 2 * DEPTH:
                value = value + (deep_high[4 + c, 3] if number else deep_high[4 + c, z - 8])
            else:
                value = value + near(3 * number + c, z)
            if number < 2:
                station[c, z + SHIFT] = value
            if -FINE_SHIFT <= z < DEPTH + FINE_SHIFT:
                anchors[3 * number + 3 + c, z + FINE_SHIFT] = value
            if 0 <= z < DEPTH:
                rows[4 * number + 3, c, z] = value

        whole = advance_halves if number else advance
        whole(start, writer(one, SHIFT), -reach - 1, reach + 5, middle, MIDDLE)
        advance(reader(one, SHIFT), store, -reach, reach + 4, middle, MIDDLE)
        start = reader(station, SHIFT)
        copy(4 * number + 3).start()

    def rest(i, carry):
        def first(c, z, value):
            one[c, z + SHIFT] = value
            if 0 <= z < DEPTH:
                rows[4 * i, c, z] = value

        def second(c, z, value):
            two[c, z + DEPTH] = value
            if 0 <= z < DEPTH:
                rows[4 * i + 1, c, z] = value

        def third(c, z, value):
            rows[4 * i + 2, c, z] = value

        advance(lambda c, z: anchors[3 * i + c, z + FINE_SHIFT], first, -2, 6, fine, FINE)
        advance(reader(one, SHIFT), second, -1, 5, fine, FINE)
        advance(reader(two), third, 0, 4, fine, FINE)
        for j in range(3):
            copy(4 * i + j).start()
        return carry

    lax.fori_loop(0, 4, rest, 0)
    for i in range(16):
        copy(i).wait()


def permute(x, moves):
    spaces = lax.axis_size("space")
    times = lax.axis_size("tm")
    pairs = []
    for t in range(times):
        if t in moves:
            target, by = moves[t]
            pairs += [(t * spaces + s, target * spaces + (s + by) % spaces) for s in range(spaces)]
        else:
            pairs += [(t * spaces + s, t * spaces + (s ^ 1)) for s in range(spaces)]
    return lax.ppermute(x, AXES, pairs)


def halos(to_up, to_down, columns, by=1):
    return (
        permute(to_up, {t: (t, by) for t in columns}),
        permute(to_down, {t: (t, -by) for t in columns}),
    )


def cycle(x, *columns):
    return permute(x, {t: (after, 0) for t, after in zip(columns, columns[1:] + columns[:1])})


PLANE = (16, 128)
WORK = pltpu.VMEM((3, 3 * DEPTH) + PLANE, jnp.float32)
VMEM_SPEC = pl.BlockSpec(memory_space=pltpu.VMEM)


def call(kernel, shapes, inputs, works, units, aliases=None, more=()):
    outs = [jax.ShapeDtypeStruct(tuple(shape) + PLANE, jnp.float32) for shape in shapes]
    result = pl.pallas_call(
        kernel,
        out_shape=outs,
        in_specs=[VMEM_SPEC] * len(inputs),
        out_specs=[VMEM_SPEC] * len(outs),
        scratch_shapes=[WORK] * works + [pltpu.VMEM(tuple(m) + PLANE, jnp.float32) for m in more],
        input_output_aliases=aliases or {},
        compiler_params=pltpu.CompilerParams(vmem_limit_bytes=8 << 20),
        cost_estimate=pl.CostEstimate(flops=units * 120000, bytes_accessed=units * 60000, transcendentals=0),
    )(*inputs)
    return result[0] if len(outs) == 1 else result


def finish(inputs):
    def work(*shape):
        return pltpu.VMEM(shape + PLANE, jnp.float32)

    wide = work(3, 2 * SHIFT + DEPTH)
    scratch = [work(16, 3, DEPTH), wide, wide, work(12, 2 * FINE_SHIFT + DEPTH), WORK]
    return pl.pallas_call(
        finish_kernel,
        name="finish",
        out_shape=jax.ShapeDtypeStruct((16, 3, DEPTH) + PLANE, jnp.float32),
        in_specs=[VMEM_SPEC] * len(inputs),
        out_specs=pl.BlockSpec(memory_space=pl.ANY),
        scratch_shapes=scratch + [pltpu.SemaphoreType.DMA((16,))],
        compiler_params=pltpu.CompilerParams(vmem_limit_bytes=8 << 20),
        cost_estimate=pl.CostEstimate(flops=20000000, bytes_accessed=4000000, transcendentals=0),
    )(*inputs)


def cycle_pass(initial, guesses, viscosity, forcing):
    times = lax.axis_size("tm")
    column = lax.axis_index("tm")
    every = range(times)
    marcher = times - 1
    alone = (marcher,)

    last, guesses = lax.optimization_barrier((guesses[3], guesses))
    members = guesses[:3].reshape((9,) + guesses.shape[2:])
    incoming = permute(last, {t: ((t + 1) % times, 0) for t in every})
    member_low, member_high = halos(members, members, every)
    fields = jnp.concatenate([forcing, viscosity[None]], axis=0)
    field_low, field_high = halos(fields, fields, every)
    opening = jnp.where(column == 0, initial, incoming)
    open_low, open_high = halos(opening, opening, every)

    table = (5, 3 * DEPTH)
    fine, middle, coarse = call(tables_kernel, [table] * 3, [field_low, fields, field_high], 0, 10)
    inputs = [member_low, members, member_high, fine, middle]
    defects, to_up, to_down = call(
        opening_kernel,
        [(1, 3, DEPTH), (3, 6), (3, 6)],
        inputs[:3] + [open_low, opening, open_high, fine, middle],
        2,
        66,
        more=[(6, 3 * DEPTH), (6, DEPTH)],
    )
    low, high = halos(to_up, to_down, every)
    others = call(defects_kernel, [(2, 3, DEPTH)], inputs, 2, 76)
    _, rest, late, deep_up, deep_down, kept = call(
        remainder_kernel,
        [(3, DEPTH)] * 2 + [(12, DEPTH)] + [(7, DEPTH)] * 2 + [(3, DEPTH)],
        [open_low, opening, open_high, middle, coarse, defects, others, to_up, initial, fields],
        1,
        20,
    )
    second_up, second_down = call(
        second_kernel, [(3, 6)] * 2, [low, to_up, high, middle, defects, others, rest], 2, 28
    )
    rest_low, rest_high = halos(second_up, second_down, every)
    term, term_middle = call(
        coarse_defect_kernel,
        [(3, 8), (3, DEPTH)],
        [rest_low, second_up, rest_high, middle, rest],
        1,
        18,
    )

    terms = {marcher: term}
    ahead = (term, term_middle)
    for t in range(min(6, marcher)):
        if t == 4:
            ahead = lax.optimization_barrier((term, term_middle, terms[0], terms[1]))
            ahead, (terms[0], terms[1]) = ahead[:2], ahead[2:]
        terms[t] = cycle(ahead[t % 2], t, marcher)
    late_low, late_high = halos(late, late, every)
    deep_low, deep_high = halos(deep_up, deep_down, every, 2)
    state, low, high = late, late_low, late_high
    brought, extra = {}, {}
    messages = None
    for period in range(times // 2):
        if period:
            low, high = halos(state, state, alone)
            for i in range(2):
                t = 2 * period + 6 + i
                done = 2 * period - 1 + i
                if period == 1 and t < marcher:
                    terms[t] = cycle(messages[i], t, marcher)
                    t -= 2
                if t < marcher:
                    terms[t] = cycle(messages[i], t, marcher, done)
                    brought[t] = done
                else:
                    extra[done] = cycle(messages[i], marcher, done)
        if 2 * period + 2 < times:
            pair = (2 * period, 2 * period + 1)
            wide = 8 if 2 * period + 8 < marcher else DEPTH
            state, *messages, kept = call(
                functools.partial(march_kernel, [brought.get(t) for t in pair]),
                [(3, DEPTH), (3, wide), (3, DEPTH), (3, DEPTH)],
                [low, state, high, coarse, terms[pair[0]], terms[pair[1]], term, kept],
                2,
                28,
                {7: 3},
            )
        else:
            start = call(
                functools.partial(last_march_kernel, [brought.get(2 * period)] + list(extra)),
                [(3, DEPTH)],
                [low, state, high, coarse, terms[2 * period], kept] + list(extra.values()),
                1,
                10,
            )

    wide = call(
        wide_table_kernel,
        [(5, 5 * DEPTH)],
        [deep_low, field_low, fields, field_high, deep_high],
        0,
        5,
    )
    lowest, highest = halos(start[:, DEPTH - 1 :], start[:, :1], every, 3)
    lower, higher = halos(start, start, every, 2)
    low, high = halos(start, start, every)
    return finish(
        [lowest, lower, low, start, high, higher, highest, fine, wide, coarse, term]
        + [deep_low, late_low, late, late_high, deep_high]
    )


def solution(mesh):
    return jax.shard_map(
        cycle_pass,
        mesh=mesh,
        in_specs=(
            P(None, "space", None, None),
            P("tm", None, "space", None, None),
            P("space", None, None),
            P(None, "space", None, None),
        ),
        out_specs=P("tm", None, "space", None, None),
        check_vma=False,
    )
```

```python
import functools

import jax
import jax.numpy as jnp
from jax import lax
from jax.experimental import pallas as pl
from jax.experimental.pallas import tpu as pltpu
from jax.sharding import PartitionSpec as P


time_step = 0.019
FINE, MIDDLE, COARSE = time_step, 2.0 * time_step, 8.0 * time_step
DEPTH = 4
AXES = ("tm", "space")


INITIAL = 4


def slab(low, own, high, base=0):
    def get(c, z):
        if z < 0:
            return low[base + c, z + DEPTH]
        if z >= DEPTH:
            return high[base + c, z - DEPTH]
        return own[base + c, z]

    return get


def deep_slab(lower, low, own, high, higher, lowest=None, highest=None):
    near = slab(low, own, high)

    def get(c, z):
        if z < -2 * DEPTH:
            return lowest[c, 0]
        if z < -DEPTH:
            return lower[c, z + 2 * DEPTH]
        if z >= 3 * DEPTH:
            return highest[c, 0]
        if z >= 2 * DEPTH:
            return higher[c, z - 2 * DEPTH]
        return near(c, z)

    return get


def reader(ref, shift=DEPTH):
    return lambda c, z: ref[c, z + shift]


def writer(ref, shift=DEPTH):
    def put(c, z, value):
        ref[c, z + shift] = value

    return put


def advance(get, put, first, last, table, step_size):
    edge = (table.shape[1] - DEPTH) // 2
    for z in range(first, last) if isinstance(first, int) else [first + i for i in range(last)]:
        alpha = table[0, z + edge]
        keep = table[1, z + edge]
        center = [get(c, z) for c in range(3)]
        half = [value * (0.5 * step_size) for value in center]
        east, west = alpha - half[0], alpha + half[0]
        north, south = alpha - half[1], alpha + half[1]
        up, down = alpha - half[2], alpha + half[2]
        for c in range(3):
            value = center[c]
            along_x = east * pltpu.roll(value, 127, 1) + west * pltpu.roll(value, 1, 1)
            along_y = north * pltpu.roll(value, 15, 0) + south * pltpu.roll(value, 1, 0)
            along_z = up * get(c, z + 1) + down * get(c, z - 1)
            put(c, z, (keep * value + table[2 + c, z + edge]) + along_x + (along_y + along_z))


def advance_halves(get, put, first, last, table, step_size):
    count = (last - first) // 2

    def body(i, carry):
        advance(get, put, first + i * count, count, table, step_size)
        return carry

    lax.fori_loop(0, 2, body, 0)


def fill(get, table, step_size):
    edge = (table.shape[1] - DEPTH) // 2
    for z in range(-edge, DEPTH + edge):
        alpha = get(3, z) * step_size
        table[0, z + edge] = alpha
        table[1, z + edge] = 1.0 - 6.0 * alpha
        for c in range(3):
            table[2 + c, z + edge] = get(c, z) * step_size


def tables_kernel(low, own, high, fine, middle, coarse):
    get = slab(low, own, high)
    for table, step_size in ((fine, FINE), (middle, MIDDLE), (coarse, COARSE)):
        fill(get, table, step_size)


def wide_table_kernel(lower, low, own, high, higher, middle):
    fill(deep_slab(lower, low, own, high, higher), middle, MIDDLE)


def defects_kernel(low, own, high, fine, middle, out, one, two):
    def body(i, carry):
        start = slab(low, own, high, 3 * (i + 1))
        advance(start, writer(one), -3, 7, fine, FINE)
        advance(reader(one), writer(two), -2, 6, fine, FINE)
        advance(reader(two), writer(one), -1, 5, fine, FINE)

        def store(c, z, value):
            out[i, c, z] = value

        def subtract(c, z, value):
            out[i, c, z] = out[i, c, z] - value

        advance(reader(one), store, 0, 4, fine, FINE)
        advance(start, writer(two), -1, 5, middle, MIDDLE)
        advance(reader(two), subtract, 0, 4, middle, MIDDLE)
        return carry

    lax.fori_loop(0, out.shape[0], body, 0)


def opening_kernel(
    member_low, members, member_high, low, own, high, fine, middle, next_one, to_up, to_down,
    one, two, both, moved,
):
    near = slab(member_low, members, member_high)
    for get, base in ((near, 0), (slab(low, own, high), 3)):
        for c in range(3):
            for z in range(-DEPTH, 2 * DEPTH):
                both[base + c, z + DEPTH] = get(c, z)

    def body(i, carry):
        def store(c, z, value):
            moved[3 * i + c, z] = value

        advance(lambda c, z: both[3 * i + c, z + DEPTH], writer(one), -3, 7, fine, FINE)
        advance(reader(one), writer(two), -2, 6, fine, FINE)
        advance(reader(two), writer(one), -1, 5, fine, FINE)
        advance(reader(one), store, 0, 4, fine, FINE)
        return carry

    lax.fori_loop(0, 2, body, 0)

    def subtract(c, z, value):
        next_one[0, c, z] = moved[c, z] - value

    advance(near, writer(one), -1, 5, middle, MIDDLE)
    advance(reader(one), subtract, 0, 4, middle, MIDDLE)
    for c in range(3):
        for z in range(DEPTH):
            to_up[c, z] = moved[3 + c, z]
            to_down[c, z] = moved[3 + c, z]
        for z in range(2):
            to_up[c, 4 + z] = next_one[0, c, 2 + z]
            to_down[c, 4 + z] = next_one[0, c, z]


def remainder_kernel(
    low, own, high, middle, coarse, next_one, others, first, fields,
    defect, rest, late, deep_up, deep_down, kept, one,
):
    start = slab(low, own, high)
    advance(start, writer(one), -1, 5, middle, MIDDLE)

    def subtract(c, z, value):
        value = first[c, z] - value
        defect[c, z] = value
        late[c, z] = value
        if z > 0:
            deep_up[4 + c, z - 1] = value
        if z < 3:
            deep_down[4 + c, z] = value

    advance(reader(one), subtract, 0, 4, middle, MIDDLE)
    advance(start, writer(one), -1, 5, coarse, COARSE)

    def subtract_rest(c, z, value):
        rest[c, z] = others[1, c, z] - value

    advance(reader(one), subtract_rest, 0, 4, coarse, COARSE)
    for c in range(3):
        for z in range(DEPTH):
            late[3 + c, z] = next_one[0, c, z]
            late[6 + c, z] = others[0, c, z]
            kept[c, z] = fields[INITIAL + c, z]
        deep_up[4 + c, 3] = next_one[0, c, 3]
        deep_down[4 + c, 3] = next_one[0, c, 0]
    for c in range(4):
        for z in range(DEPTH):
            deep_up[c, z] = fields[c, z]
            deep_down[c, z] = fields[c, z]


def second_kernel(low, own, high, middle, defects, others, rest, to_up, to_down, one, two):
    def added(c, z, value):
        if z < 0:
            term = low[c, 4 + 2 + z]
        elif z >= DEPTH:
            term = high[c, 4 + z - DEPTH]
        else:
            term = defects[0, c, z]
        two[c, z + DEPTH] = value + term

    def third(c, z, value):
        value = value + others[0, c, z]
        to_up[c, z] = value
        to_down[c, z] = value

    advance(slab(low, own, high), writer(one), -3, 7, middle, MIDDLE)
    advance(reader(one), added, -2, 6, middle, MIDDLE)
    advance(reader(two), writer(one), -1, 5, middle, MIDDLE)
    advance(reader(one), third, 0, 4, middle, MIDDLE)
    for c in range(3):
        for z in range(2):
            to_up[c, 4 + z] = rest[c, 2 + z]
            to_down[c, 4 + z] = rest[c, z]


def coarse_defect_kernel(low, own, high, middle, rest, out, middle_out, one):
    def added(c, z, value):
        if z < 0:
            term = low[c, 4 + 2 + z]
        elif z >= DEPTH:
            term = high[c, 4 + z - DEPTH]
        else:
            term = rest[c, z]
        out[c, z + 2] = value + term
        if 0 <= z < DEPTH:
            middle_out[c, z] = value + term

    advance(slab(low, own, high), writer(one), -3, 7, middle, MIDDLE)
    advance(reader(one), added, -2, 6, middle, MIDDLE)


def take(kept, arrived):
    shift = (arrived.shape[1] - DEPTH) // 2
    for c in range(3):
        for z in range(DEPTH):
            kept[c, z] = arrived[c, z + shift]


def march_kernel(
    base, done, low, own, high, coarse, term_one, term_two, term, kept_in,
    state, message_one, message_two, kept, one, two,
):
    def first(c, z, value):
        value = value + term_one[c, z + 2]
        two[c, z + DEPTH] = value
        if 0 <= z + edge < message_one.shape[1]:
            message_one[c, z + edge] = value

    def second(c, z, value):
        value = value + term_two[c, z]
        state[c, z] = value
        message_two[c, z] = value

    edge = (message_one.shape[1] - DEPTH) // 2
    column = lax.axis_index("tm")
    marching = column == lax.axis_size("tm") - 1

    @pl.when(marching)
    def _():
        advance(slab(low, own, high, base), writer(one), -3, 7, coarse, COARSE)
        advance(reader(one), first, -2, 6, coarse, COARSE)
        advance(reader(two), writer(one), -1, 5, coarse, COARSE)
        advance(reader(one), second, 0, 4, coarse, COARSE)

    @pl.when(jnp.logical_not(marching))
    def _():
        for c in range(3):
            for z in range(message_one.shape[1]):
                message_one[c, z] = term[c, z + 2 - edge]
            for z in range(DEPTH):
                message_two[c, z] = term[c, z + 2]
                state[c, z] = own[base + c, z]
                kept[c, z] = kept_in[c, z]

    if done[0] is not None:
        pl.when(column == done[0])(functools.partial(take, kept, term_one))
    if done[1] is not None:
        pl.when(column == done[1])(functools.partial(take, kept, term_two))


def last_march_kernel(done, low, own, high, coarse, term_one, kept, *rest):
    arrivals, (start, one) = rest[:-2], rest[-2:]
    column = lax.axis_index("tm")
    marching = column == lax.axis_size("tm") - 1

    def first(c, z, value):
        start[c, z] = value + term_one[c, z + 2]

    @pl.when(marching)
    def _():
        advance(slab(low, own, high), writer(one), -1, 5, coarse, COARSE)
        advance(reader(one), first, 0, 4, coarse, COARSE)

    pl.when(jnp.logical_not(marching))(functools.partial(take, start, kept))
    for t, arrived in zip(done, (term_one,) + arrivals):
        if t is not None:
            pl.when(column == t)(functools.partial(take, start, arrived))


SHIFT = 2 * DEPTH + 2
FINE_SHIFT = 3


def finish_kernel(
    lowest, lower, low, own, high, higher, highest, fine, middle, coarse, term,
    deep_low, late_low, late, late_high, deep_high, result, rows, one, station, anchors, two, sem,
):
    def copy(i):
        return pltpu.make_async_copy(rows.at[i], result.at[i], sem.at[i])

    start = deep_slab(lower, low, own, high, higher, lowest, highest)
    near = slab(late_low, late, late_high)
    for c in range(3):
        for z in range(-FINE_SHIFT, DEPTH + FINE_SHIFT):
            anchors[c, z + FINE_SHIFT] = start(c, z)

    def end(c, z, value):
        rows[15, c, z] = value + term[c, z + 2]

    advance(start, writer(one, SHIFT), -1, 5, coarse, COARSE)
    advance(reader(one, SHIFT), end, 0, 4, coarse, COARSE)
    copy(15).start()

    for number in range(3):
        reach = 7 - 2 * number

        def store(c, z, value):
            if z < -DEPTH:
                value = value + (deep_low[4 + c, 3] if number else deep_low[4 + c, z + 7])
            elif z >= 2 * DEPTH:
                value = value + (deep_high[4 + c, 3] if number else deep_high[4 + c, z - 8])
            else:
                value = value + near(3 * number + c, z)
            if number < 2:
                station[c, z + SHIFT] = value
            if -FINE_SHIFT <= z < DEPTH + FINE_SHIFT:
                anchors[3 * number + 3 + c, z + FINE_SHIFT] = value
            if 0 <= z < DEPTH:
                rows[4 * number + 3, c, z] = value

        whole = advance_halves if number else advance
        whole(start, writer(one, SHIFT), -reach - 1, reach + 5, middle, MIDDLE)
        advance(reader(one, SHIFT), store, -reach, reach + 4, middle, MIDDLE)
        start = reader(station, SHIFT)
        copy(4 * number + 3).start()

    def rest(i, carry):
        def first(c, z, value):
            one[c, z + SHIFT] = value
            if 0 <= z < DEPTH:
                rows[4 * i, c, z] = value

        def second(c, z, value):
            two[c, z + DEPTH] = value
            if 0 <= z < DEPTH:
                rows[4 * i + 1, c, z] = value

        def third(c, z, value):
            rows[4 * i + 2, c, z] = value

        advance(lambda c, z: anchors[3 * i + c, z + FINE_SHIFT], first, -2, 6, fine, FINE)
        advance(reader(one, SHIFT), second, -1, 5, fine, FINE)
        advance(reader(two), third, 0, 4, fine, FINE)
        for j in range(3):
            copy(4 * i + j).start()
        return carry

    lax.fori_loop(0, 4, rest, 0)
    for i in range(16):
        copy(i).wait()


def permute(x, moves):
    spaces = lax.axis_size("space")
    times = lax.axis_size("tm")
    pairs = []
    for t in range(times):
        if t in moves:
            target, by = moves[t]
            pairs += [(t * spaces + s, target * spaces + (s + by) % spaces) for s in range(spaces)]
        else:
            pairs += [(t * spaces + s, t * spaces + (s ^ 1)) for s in range(spaces)]
    return lax.ppermute(x, AXES, pairs)


def halos(to_up, to_down, columns, by=1):
    return (
        permute(to_up, {t: (t, by) for t in columns}),
        permute(to_down, {t: (t, -by) for t in columns}),
    )


def cycle(x, *columns):
    return permute(x, {t: (after, 0) for t, after in zip(columns, columns[1:] + columns[:1])})


PLANE = (16, 128)
WORK = pltpu.VMEM((3, 3 * DEPTH) + PLANE, jnp.float32)
VMEM_SPEC = pl.BlockSpec(memory_space=pltpu.VMEM)


def call(kernel, shapes, inputs, works, units, more=()):
    outs = [jax.ShapeDtypeStruct(tuple(shape) + PLANE, jnp.float32) for shape in shapes]
    result = pl.pallas_call(
        kernel,
        out_shape=outs,
        in_specs=[VMEM_SPEC] * len(inputs),
        out_specs=[VMEM_SPEC] * len(outs),
        scratch_shapes=[WORK] * works + [pltpu.VMEM(tuple(m) + PLANE, jnp.float32) for m in more],
        compiler_params=pltpu.CompilerParams(vmem_limit_bytes=8 << 20),
        cost_estimate=pl.CostEstimate(flops=units * 120000, bytes_accessed=units * 60000, transcendentals=0),
    )(*inputs)
    return result[0] if len(outs) == 1 else result


def finish(inputs):
    def work(*shape):
        return pltpu.VMEM(shape + PLANE, jnp.float32)

    wide = work(3, 2 * SHIFT + DEPTH)
    scratch = [work(16, 3, DEPTH), wide, wide, work(12, 2 * FINE_SHIFT + DEPTH), WORK]
    return pl.pallas_call(
        finish_kernel,
        name="finish",
        out_shape=jax.ShapeDtypeStruct((16, 3, DEPTH) + PLANE, jnp.float32),
        in_specs=[VMEM_SPEC] * len(inputs),
        out_specs=pl.BlockSpec(memory_space=pl.ANY),
        scratch_shapes=scratch + [pltpu.SemaphoreType.DMA((16,))],
        compiler_params=pltpu.CompilerParams(vmem_limit_bytes=8 << 20),
        cost_estimate=pl.CostEstimate(flops=20000000, bytes_accessed=4000000, transcendentals=0),
    )(*inputs)


def cycle_pass(initial, guesses, viscosity, forcing):
    times = lax.axis_size("tm")
    column = lax.axis_index("tm")
    every = range(times)
    marcher = times - 1
    alone = (marcher,)

    last, guesses = lax.optimization_barrier((guesses[3], guesses))
    members = guesses[:3].reshape((9,) + guesses.shape[2:])
    incoming = permute(last, {t: ((t + 1) % times, 0) for t in every})
    member_low, member_high = halos(members, members, every)
    fields = jnp.concatenate([forcing, viscosity[None], initial], axis=0)
    field_low, field_high = halos(fields, fields, every)
    opening = jnp.where(column == 0, initial, incoming)
    open_low, open_high = halos(opening, opening, every)

    table = (5, 3 * DEPTH)
    fine, middle, coarse = call(tables_kernel, [table] * 3, [field_low, fields, field_high], 0, 10)
    inputs = [member_low, members, member_high, fine, middle]
    defects, to_up, to_down = call(
        opening_kernel,
        [(1, 3, DEPTH), (3, 6), (3, 6)],
        inputs[:3] + [open_low, opening, open_high, fine, middle],
        2,
        66,
        more=[(6, 3 * DEPTH), (6, DEPTH)],
    )
    low, high = halos(to_up, to_down, every)
    others = call(defects_kernel, [(2, 3, DEPTH)], inputs, 2, 76)
    _, rest, late, deep_up, deep_down, kept = call(
        remainder_kernel,
        [(3, DEPTH)] * 2 + [(9, DEPTH)] + [(7, DEPTH)] * 2 + [(3, DEPTH)],
        [open_low, opening, open_high, middle, coarse, defects, others, to_up, fields],
        1,
        20,
    )
    second_up, second_down = call(
        second_kernel, [(3, 6)] * 2, [low, to_up, high, middle, defects, others, rest], 2, 28
    )
    rest_low, rest_high = halos(second_up, second_down, every)
    term, term_middle = call(
        coarse_defect_kernel,
        [(3, 8), (3, DEPTH)],
        [rest_low, second_up, rest_high, middle, rest],
        1,
        18,
    )

    terms = {marcher: term}
    ahead = (term, term_middle)
    for t in range(min(6, marcher)):
        if t == 4:
            ahead = lax.optimization_barrier((term, term_middle, terms[0], terms[1]))
            ahead, (terms[0], terms[1]) = ahead[:2], ahead[2:]
        terms[t] = cycle(ahead[t % 2], t, marcher)
    late_low, late_high = halos(late, late, every)
    deep_low, deep_high = halos(deep_up, deep_down, every, 2)
    state, low, high = fields, field_low, field_high
    brought, extra = {}, {}
    messages = None
    for period in range(times // 2):
        if period:
            low, high = halos(state, state, alone)
            for i in range(2):
                t = 2 * period + 6 + i
                done = 2 * period - 1 + i
                if period == 1 and t < marcher:
                    terms[t] = cycle(messages[i], t, marcher)
                    t -= 2
                if t < marcher:
                    terms[t] = cycle(messages[i], t, marcher, done)
                    brought[t] = done
                else:
                    extra[done] = cycle(messages[i], marcher, done)
        if 2 * period + 2 < times:
            pair = (2 * period, 2 * period + 1)
            wide = 8 if 2 * period + 8 < marcher else DEPTH
            state, *messages, kept = call(
                functools.partial(march_kernel, 0 if period else INITIAL, [brought.get(t) for t in pair]),
                [(3, DEPTH), (3, wide), (3, DEPTH), (3, DEPTH)],
                [low, state, high, coarse, terms[pair[0]], terms[pair[1]], term, kept],
                2,
                28,
            )
        else:
            start = call(
                functools.partial(last_march_kernel, [brought.get(2 * period)] + list(extra)),
                [(3, DEPTH)],
                [low, state, high, coarse, terms[2 * period], kept] + list(extra.values()),
                1,
                10,
            )

    wide = call(
        wide_table_kernel,
        [(5, 5 * DEPTH)],
        [deep_low, field_low, fields, field_high, deep_high],
        0,
        5,
    )
    lowest, highest = halos(start[:, DEPTH - 1 :], start[:, :1], every, 3)
    lower, higher = halos(start, start, every, 2)
    low, high = halos(start, start, every)
    return finish(
        [lowest, lower, low, start, high, higher, highest, fine, wide, coarse, term]
        + [deep_low, late_low, late, late_high, deep_high]
    )


def solution(mesh):
    return jax.shard_map(
        cycle_pass,
        mesh=mesh,
        in_specs=(
            P(None, "space", None, None),
            P("tm", None, "space", None, None),
            P("space", None, None),
            P(None, "space", None, None),
        ),
        out_specs=P("tm", None, "space", None, None),
        check_vma=False,
    )
```
